256 devices in a mesh: row: 16 (over z, core), col: 16 (over x, y).
Axes of the slice: x: 4, y: 4, z: 8, core: 2. Of those that a mesh axis runs over, the one named last changes fastest.
Arguments:
- targets: float32 [3, 131072], P(None, 'row'), may hold values from 0 to 1, as said below
- sources: float32 [3, 32768], P(None, 'col'), may hold values from 0 to 1, as said below
- samples: bfloat16 [32768, 128], P('col', 'row'), may hold values from -0.03125 to 0.03125
- near: int32 [256, 8], P('row'), may hold values from -1 to 63, as said below
Outputs:
- leaf_bases: float32 [131072, 128], P(('row', 'col'))
- nested: float32 [131072, 128], P(('row', 'col'))
The draws below stay inside these ranges and needn't reach their ends.
Inputs may be any that keep to these rules, and one draw needn't show every extreme that they name: `near`: in each row, entries after the first -1 are -1 and the first entry is a source leaf; a row may name a source leaf twice. `targets`: the points of one leaf lie about a common centre. `sources`: the points of one leaf lie about a common centre.
All inputs are finite; a program needn't handle non-finite values.
Results may differ from the reference program's by a relative error of at most 0.0071.
Values may be sent and summed in bfloat16 or wider, within the bound.
No kernel may reach another device: no remote copies, remote signals or barrier semaphores. Data moves between devices by JAX's collectives and lax.ppermute only.
A program may use at most 64 MiB of HBM per device.

```python
import jax
import jax.numpy as jnp
from jax import lax

R = 128
LEAF = 512
NEAR = 8
ROWS = 131072
COLS = 32768
LEAVES = 256
CLEAVES = 64


def morton_cells(count):
    total_bits = max(1, (count - 1).bit_length())
    index_all = jnp.arange(count).astype(jnp.int32)
    coords = []
    widths = []
    for axis_pick in range(3):
        value = jnp.zeros((count,), jnp.int32)
        level = 0
        for bit_pos in range(total_bits):
            if bit_pos % 3 == axis_pick:
                value = value + (index_all >> bit_pos & 1) * 2 ** level
                level = level + 1
        coords.append(value)
        widths.append(level)
    return (coords, widths)


def clustered_points(key, count):
    coords, widths = morton_cells(count)
    noise = jax.random.normal(key, (3, count, LEAF), dtype=jnp.float32)
    rows_out = []
    for axis_pick in range(3):
        cell_size = 1.0 / 2 ** widths[axis_pick]
        centre = (coords[axis_pick].astype(jnp.float32) + 0.5) * cell_size
        spread = centre[:, None] + 0.35 * cell_size * noise[axis_pick]
        rows_out.append(jnp.clip(spread, 0.0, 1.0).reshape(count * LEAF))
    return jnp.stack(rows_out, axis=0).astype(jnp.float32)


def draw_targets(key, part):
    return clustered_points(jax.random.fold_in(key, 21), LEAVES)


def draw_sources(key, part):
    return clustered_points(jax.random.fold_in(key, 22), CLEAVES)


def draw_near(key, part):
    key_ties, key_counts = jax.random.split(jax.random.fold_in(key, 11))
    target_coords, target_widths = morton_cells(LEAVES)
    source_coords, source_widths = morton_cells(CLEAVES)
    finest = max(target_widths + source_widths) + 1
    dist_sq = jnp.zeros((LEAVES, CLEAVES), jnp.int32)
    for axis_pick in range(3):
        target_pos = (2 * target_coords[axis_pick] + 1) * 2 ** (finest - target_widths[axis_pick] - 1)
        source_pos = (2 * source_coords[axis_pick] + 1) * 2 ** (finest - source_widths[axis_pick] - 1)
        gap = target_pos[:, None] - source_pos[None, :]
        dist_sq = dist_sq + gap * gap
    offsets = jax.random.randint(key_ties, (LEAVES, 1), 0, CLEAVES)
    ties = (offsets + jnp.arange(CLEAVES).astype(jnp.int32)[None, :]) % CLEAVES
    scores = dist_sq * CLEAVES + ties
    unused, nearest = lax_top(-scores)
    nearest = nearest.astype(jnp.int32)
    nearest = nearest.at[0, 1].set(nearest[0, 0])
    counts_drawn = jax.random.randint(key_counts, (LEAVES,), 1, NEAR + 1)
    counts_drawn = counts_drawn.at[0].set(NEAR).at[1].set(1)
    slots_index = jnp.arange(NEAR)
    return jnp.where(slots_index[None, :] < counts_drawn[:, None], nearest, -1).astype(jnp.int32)


def lax_top(scores):
    return jax.lax.top_k(scores, NEAR)


def shard_levels(key, extent, pieces, low, top_value):
    loudness, own = 1.0, jax.random.fold_in(key, 6)
    for dim, blocks in pieces:
        steps = jnp.exp(jax.random.uniform(jax.random.fold_in(own, dim), (blocks,), jnp.float32, low / len(pieces), top_value / len(pieces)))
        loudness = loudness * jnp.repeat(steps, extent[dim] // blocks).reshape([-1 if axis == dim else 1 for axis in range(len(extent))])
    return loudness


def centred(key, dims, deviation, limit, pieces=(), kind=jnp.bfloat16):
    entries = deviation * jax.random.normal(key, dims, jnp.float32)
    if pieces:
        entries = entries * shard_levels(key, dims, pieces, -0.22, 0.18)
    return jnp.clip(entries, -limit, limit).astype(kind)


def setup_inputs(seed: int = 0) -> dict:
    streams_of = jax.random.split(jax.random.key(seed), 5)
    return {
        "targets": draw_targets(jax.random.fold_in(streams_of[4], 71), 0),
        "sources": draw_sources(jax.random.fold_in(streams_of[4], 71), 0),
        "samples": centred(streams_of[2], (COLS, R), COLS ** -0.5, 0.03125, ((0, 16), (1, 16))),
        "near": draw_near(jax.random.fold_in(streams_of[4], 71), 0),
    }


corr_length = 0.1
ridge = 0.1

def kernel_block(points, others):
    dist_sq = (points[0][:, None] - others[0][None, :]) ** 2
    dist_sq = dist_sq + (points[1][:, None] - others[1][None, :]) ** 2
    dist_sq = dist_sq + (points[2][:, None] - others[2][None, :]) ** 2
    return jnp.exp(-jnp.sqrt(dist_sq) / corr_length)

def basis(stacked):
    row_count = stacked.shape[0]
    rank_width = stacked.shape[1]
    gram_matrix = jnp.matmul(stacked.T, stacked, precision=lax.Precision.HIGHEST) / row_count
    ridge_term = ridge * jnp.trace(gram_matrix) / rank_width
    factor = jnp.linalg.cholesky(gram_matrix + ridge_term * jnp.eye(rank_width, dtype=gram_matrix.dtype))
    bases = lax.linalg.triangular_solve(factor, stacked, left_side=False, lower=True, transpose_a=True)
    projected = jnp.matmul(bases.T, stacked, precision=lax.Precision.HIGHEST) / row_count
    return (bases, projected)

def reference(targets, sources, samples, near):
    leaf_total = ROWS // LEAF
    col_leaf = (jnp.arange(COLS) // LEAF).astype(jnp.int32)

    def leaf_sample(inputs):
        points, near_row = inputs
        near_hits = jnp.any(near_row[:, None] == col_leaf[None, :], axis=0)
        keep_mask = jnp.where(near_hits, 0.0, 1.0).astype(jnp.float32)
        kernel_tile = (kernel_block(points, sources) * keep_mask[None, :]).astype(jnp.bfloat16)
        return jnp.dot(kernel_tile.astype(jnp.float32), samples.astype(jnp.float32), preferred_element_type=jnp.float32)
    points_all = targets.reshape(3, leaf_total, LEAF).transpose(1, 0, 2)
    far_sample = lax.map(leaf_sample, (points_all, near))
    leaf_basis, proj_zero = jax.vmap(basis)(far_sample)
    upper_one, proj_one = jax.vmap(basis)(proj_zero.reshape(leaf_total // 2, 2 * R, R))
    upper_two, unused = jax.vmap(basis)(proj_one.reshape(leaf_total // 4, 2 * R, R))
    own_one = upper_one.reshape(leaf_total, R, R)
    own_two = jnp.repeat(upper_two.reshape(leaf_total // 2, R, R), 2, axis=0)
    first = jnp.einsum('lab,lbc->lac', leaf_basis, own_one, precision=lax.Precision.HIGHEST)
    nested = jnp.einsum('lab,lbc->lac', first, own_two, precision=lax.Precision.HIGHEST) / R
    return (leaf_basis.reshape(ROWS, R), nested.reshape(ROWS, R))
```

```python
import jax
import jax.numpy as jnp
from jax import lax
from jax.sharding import Mesh
from jax.sharding import PartitionSpec as P
from jax.experimental import pallas as pl
from jax.experimental.pallas import tpu as pltpu

LEAF = 512
corr_length = 0.1
ridge = 0.1
LOG2E = 1.4426950408889634
HI = lax.Precision.HIGHEST
F32 = jnp.float32
BF = jnp.bfloat16


def parts3(x):
    a = x.astype(BF).astype(F32)
    rest = x - a
    b = rest.astype(BF).astype(F32)
    return a, b, rest - b


def features(points, centre, source):
    row = lax.broadcasted_iota(jnp.int32, points.shape, 0)
    shift = jnp.where(row < 3, (points - centre) * (LOG2E / corr_length), 0.0)
    norm = jnp.sum(shift * shift, axis=0, keepdims=True)
    if source:
        full = jnp.where(row == 3, norm, jnp.where(row == 4, 1.0, shift))
        a, b, c = parts3(full)
        stack = [a, b, a, c, b, a]
    else:
        full = jnp.where(row == 4, norm, jnp.where(row == 3, 1.0, -2.0 * shift))
        a, b, c = parts3(full)
        stack = [a, a, b, a, b, c]
    return jnp.concatenate(stack, axis=0).astype(BF)


def kernel_tile(lhs, rhs):
    d2 = lax.dot_general(lhs, rhs, (((0,), (0,)), ((), ())), preferred_element_type=F32)
    d2 = jnp.maximum(d2, 1e-24)
    return jnp.exp2(-(d2 * lax.rsqrt(d2))).astype(BF)


def far_body(width, keep_ref, tgt_ref, src_ref, smp_ref, out_ref, rhs_ref, lhs_ref):
    leaf = pl.program_id(0)
    pts = tgt_ref[...]
    centre = jnp.mean(pts, axis=1, keepdims=True)
    lhs_ref[...] = features(pts, centre, False)
    rhs_ref[...] = features(src_ref[...], centre, True)
    out_ref[...] = jnp.zeros_like(out_ref)
    per = LEAF // width

    def step(i, carry):
        @pl.when(keep_ref[leaf, i // per] != 0)
        def _():
            start = pl.multiple_of(i * width, width)
            tile = kernel_tile(lhs_ref[...], rhs_ref[:, pl.ds(start, width)])
            out_ref[...] += jnp.dot(tile, smp_ref[pl.ds(start, width), :], preferred_element_type=F32)
        return carry

    lax.fori_loop(0, src_ref.shape[1] // width, step, 0)


def far_sums(keep, targets8, sources8, samples, width=512):
    leaves = targets8.shape[1] // LEAF
    cols = sources8.shape[1]
    import functools
    return pl.pallas_call(
        functools.partial(far_body, width),
        out_shape=jax.ShapeDtypeStruct((leaves * LEAF, 128), F32),
        grid_spec=pltpu.PrefetchScalarGridSpec(
            num_scalar_prefetch=1,
            grid=(leaves,),
            in_specs=[
                pl.BlockSpec((8, LEAF), lambda i, k: (0, i)),
                pl.BlockSpec((8, cols), lambda i, k: (0, 0)),
                pl.BlockSpec((cols, 128), lambda i, k: (0, 0)),
            ],
            out_specs=pl.BlockSpec((LEAF, 128), lambda i, k: (i, 0)),
            scratch_shapes=[pltpu.VMEM((48, cols), BF), pltpu.VMEM((48, LEAF), BF)],
        ),
        name="far_sums",
    )(keep, targets8, sources8, samples)


def eliminate(gram, aug_ref, top_ref):
    n = 128
    i = lax.broadcasted_iota(jnp.int32, (n, n), 0)
    j = lax.broadcasted_iota(jnp.int32, (n, n), 1)
    aug_ref[:, :n] = gram
    aug_ref[:, n:] = jnp.where(i == j, 1.0, 0.0)
    sub = lax.broadcasted_iota(jnp.int32, (8, n), 0)
    lane = lax.broadcasted_iota(jnp.int32, (8, n), 1)
    for b in range(n // 8):
        at = 8 * b
        left = aug_ref[at:at + 8, :n]
        right = aug_ref[at:at + 8, n:]
        cols = [jnp.broadcast_to(left[:, at + k:at + k + 1], (8, n)) for k in range(8)]
        scale = jnp.zeros((8, n), F32)
        for k in range(8):
            piv = jnp.broadcast_to(cols[k][k:k + 1, :], (8, n))
            inv = lax.rsqrt(piv)
            scale = jnp.where(sub == k, inv, scale)
            if k < 7:
                mult = jnp.where(sub > k, cols[k] * (inv * inv), 0.0)
                for q in range(k + 1, 8):
                    cols[q] = cols[q] - mult * jnp.broadcast_to(cols[q][k:k + 1, :], (8, n))
                left = left - mult * jnp.broadcast_to(left[k:k + 1, :], (8, n))
                right = right - mult * jnp.broadcast_to(right[k:k + 1, :], (8, n))
        left = jnp.where(lane >= sub + at, left * scale, 0.0)
        right = right * scale
        top_ref[at:at + 8, :n] = left
        top_ref[at:at + 8, n:] = right
        if b < n // 8 - 1:
            l1, l2, l3 = parts3(left)
            r1, r2, r3 = parts3(right)
            lhs = jnp.concatenate([l1, l1, l2, l1, l2, l3], axis=0).astype(BF)
            rl = jnp.concatenate([l1, l2, l1, l3, l2, l1], axis=0)
            rr = jnp.concatenate([r1, r2, r1, r3, r2, r1], axis=0)
            rhs = jnp.concatenate([rl, rr], axis=1).astype(BF)
            upd = lax.dot_general(lhs, rhs, (((0,), (0,)), ((), ())), preferred_element_type=F32)
            aug_ref[at + 8:, :] -= upd[at + 8:, :]


def regular(gram):
    i = lax.broadcasted_iota(jnp.int32, gram.shape, 0)
    j = lax.broadcasted_iota(jnp.int32, gram.shape, 1)
    diag = jnp.where(i == j, gram, 0.0)
    lam = (ridge / gram.shape[0]) * jnp.sum(jnp.sum(diag, axis=1, keepdims=True), axis=0, keepdims=True)
    return gram + jnp.where(i == j, lam, 0.0), lam


def tdot(a, b):
    return lax.dot_general(a, b, (((0,), (0,)), ((), ())), precision=HI, preferred_element_type=F32)


def ndot(a, b):
    return lax.dot_general(a, b, (((1,), (1,)), ((), ())), precision=HI, preferred_element_type=F32)


def mdot(a, b):
    return lax.dot_general(a, b, (((1,), (0,)), ((), ())), precision=HI, preferred_element_type=F32)


def leaf_body(z_ref, inv_ref, proj_ref, sq_ref, aug_ref, top_ref):
    z = z_ref[...]
    gram, lam = regular(tdot(z, z) * (1.0 / z.shape[0]))
    eliminate(gram, aug_ref, top_ref)
    inv = top_ref[:, 128:]
    proj = top_ref[:, :128] - lam * inv
    inv_ref[...] = inv
    proj_ref[...] = proj
    sq_ref[...] = tdot(proj, proj)


def node_body(a_ref, b_ref, inv_ref, proj_ref, sq_ref, aug_ref, top_ref):
    gram, lam = regular((a_ref[...] + b_ref[...]) * (1.0 / 256))
    eliminate(gram, aug_ref, top_ref)
    inv = top_ref[:, 128:]
    proj = top_ref[:, :128] - lam * inv
    inv_ref[...] = inv
    proj_ref[...] = proj
    sq_ref[...] = tdot(proj, proj)


def carry_body(z_ref, inv_ref, proj_ref, base_ref, next_ref):
    base = ndot(z_ref[...], inv_ref[...])
    base_ref[...] = base
    next_ref[...] = mdot(base, proj_ref[...])


def carry2_body(z_ref, inv_ref, proj_ref, next_ref):
    next_ref[...] = mdot(ndot(z_ref[...], inv_ref[...]), proj_ref[...])


def last_body(a_ref, b_ref, z_ref, out_ref, aug_ref, top_ref):
    gram, lam = regular((a_ref[...] + b_ref[...]) * (1.0 / 256))
    eliminate(gram, aug_ref, top_ref)
    out_ref[...] = ndot(z_ref[...], top_ref[:, 128:]) * (1.0 / 128)


def sds(*shape):
    return jax.ShapeDtypeStruct(shape, F32)


SCR = [pltpu.VMEM((128, 256), F32), pltpu.VMEM((128, 256), F32)]


def cost(f):
    return pl.CostEstimate(flops=f, bytes_accessed=400000, transcendentals=0)


def leaf_node(z):
    return pl.pallas_call(leaf_body, out_shape=(sds(128, 128),) * 3, scratch_shapes=SCR, name="leaf_node")(z)


def pair_node(a, b):
    return pl.pallas_call(node_body, out_shape=(sds(128, 128),) * 3, scratch_shapes=SCR, name="pair_node")(a, b)


def carry(z, inv, proj):
    return pl.pallas_call(carry_body, out_shape=(sds(512, 128),) * 2, name="carry")(z, inv, proj)


def carry2(z, inv, proj):
    return pl.pallas_call(carry2_body, out_shape=sds(512, 128), name="carry2")(z, inv, proj)


def last_node(a, b, z):
    return pl.pallas_call(last_body, out_shape=sds(512, 128), scratch_shapes=SCR, name="last_node")(a, b, z)


ROW = ("row_0", "row_1")
ROW_COL = ("row_0", "row_1", "col")


def gathered_by_axis(x, axes, dim):
    if not axes:
        return x
    nearer = lax.all_gather(x, axes[-1], axis=dim, tiled=True)
    return gathered_by_axis(nearer, axes[:-1], dim)


def split_up(x, dim, size):
    before, after = (x.shape[:dim], x.shape[dim + 1:])
    return jnp.moveaxis(x.reshape(*before, size, -1, *after), dim, 0)


def sent_and_summed(x, axis, dim):
    size = lax.axis_size(axis)
    parts = lax.all_to_all(split_up(x, dim, size), axis, 0, 0, tiled=True)
    return jnp.sum(parts, axis=0)


def partner(x, axis, apart):
    return lax.ppermute(x, axis, [(i, i ^ 1 << apart) for i in range(lax.axis_size(axis))])


def per_device(targets, sources, samples, near):
    sample_cols = gathered_by_axis(samples, ROW, 1)
    col_index = lax.axis_index("col")
    col_leaves = sources.shape[1] // LEAF
    local_ids = col_index * col_leaves + jnp.arange(col_leaves)
    near_hits = jnp.any(near[:, :, None] == local_ids[None, None, :], axis=1)
    keep = jnp.where(near_hits, 0, 1).astype(jnp.int32)
    pad = lambda x: jnp.pad(x, ((0, 5), (0, 0)))
    products = far_sums(keep, pad(targets), pad(sources), sample_cols)
    far_sample = sent_and_summed(products, "col", 0)
    inv0, proj0, sq0 = leaf_node(far_sample)
    sib = partner(sq0, "col", 0)
    leaf_basis, carried = carry(far_sample, inv0, proj0)
    inv1, proj1, sq1 = pair_node(sq0, sib)
    cousin = partner(sq1, "col", 1)
    carried = carry2(carried, inv1, proj1)
    nested = last_node(sq1, cousin, carried)
    return (leaf_basis, nested)


def solution(mesh):
    torus = Mesh(mesh.devices.reshape(8, 2, mesh.shape["col"]), ("row_0", "row_1", "col"))
    placed = (P(None, ROW), P(None, "col"), P("col", ROW), P(ROW, None))
    return jax.shard_map(
        per_device,
        mesh=torus,
        in_specs=placed,
        out_specs=(P(ROW_COL, None), P(ROW_COL, None)),
        check_vma=False,
    )
```

```python
import jax
import jax.numpy as jnp
from jax import lax
from jax.sharding import Mesh
from jax.sharding import PartitionSpec as P
from jax.experimental import pallas as pl
from jax.experimental.pallas import tpu as pltpu

LEAF = 512
corr_length = 0.1
ridge = 0.1
LOG2E = 1.4426950408889634
HI = lax.Precision.HIGHEST
F32 = jnp.float32
BF = jnp.bfloat16


def parts3(x):
    a = x.astype(BF).astype(F32)
    rest = x - a
    b = rest.astype(BF).astype(F32)
    return a, b, rest - b


def features(points, centre, source, masked=0.0):
    row = lax.broadcasted_iota(jnp.int32, points.shape, 0)
    shift = jnp.where(row < 3, (points - centre) * (LOG2E / corr_length), 0.0)
    norm = jnp.sum(shift * shift, axis=0, keepdims=True) + masked
    if source:
        full = jnp.where(row == 3, norm, jnp.where(row == 4, 1.0, shift))
        a, b, c = parts3(full)
        stack = [a, b, a, c, b, a]
    else:
        full = jnp.where(row == 4, norm, jnp.where(row == 3, 1.0, -2.0 * shift))
        a, b, c = parts3(full)
        stack = [a, a, b, a, b, c]
    return jnp.concatenate(stack, axis=0).astype(BF)


def kernel_tile(lhs, rhs):
    d2 = lax.dot_general(lhs, rhs, (((0,), (0,)), ((), ())), preferred_element_type=F32)
    d2 = jnp.maximum(d2, 1e-24)
    return jnp.exp2(-(d2 * lax.rsqrt(d2))).astype(BF)


def tiles_body(keep_ref, tgt_ref, src_ref, out_ref):
    leaf = pl.program_id(0)
    pts = tgt_ref[...]
    centre = jnp.mean(pts, axis=1, keepdims=True)
    lhs = features(pts, centre, False)
    for i in range(src_ref.shape[1] // LEAF):
        at = slice(i * LEAF, (i + 1) * LEAF)
        away = jnp.where(keep_ref[leaf, i] != 0, 0.0, 1e9)
        rhs = features(src_ref[:, at], centre, True, away)
        out_ref[:, at] = kernel_tile(lhs, rhs)


def kernel_tiles(keep, targets8, sources8):
    rows, cols = targets8.shape[1], sources8.shape[1]
    return pl.pallas_call(
        tiles_body,
        out_shape=jax.ShapeDtypeStruct((rows, cols), BF),
        grid_spec=pltpu.PrefetchScalarGridSpec(
            num_scalar_prefetch=1,
            grid=(rows // LEAF,),
            in_specs=[
                pl.BlockSpec((8, LEAF), lambda i, k: (0, i)),
                pl.BlockSpec((8, cols), lambda i, k: (0, 0)),
            ],
            out_specs=pl.BlockSpec((LEAF, cols), lambda i, k: (i, 0)),
        ),
        cost_estimate=pl.CostEstimate(flops=8_000_000_000, bytes_accessed=2 * rows * cols, transcendentals=2 * rows * cols),
        name="kernel_tiles",
    )(keep, targets8, sources8)


def prep_body(where_ref, mine_ref, other_ref, out_ref):
    z, c = where_ref[0], where_ref[1]
    for ref, half in ((mine_ref, c), (other_ref, 1 - c)):
        rows = jnp.concatenate([ref[jnp.bitwise_xor(z, p)] for p in range(8)], axis=0)
        start = pl.multiple_of(half * 1024, 1024)
        out_ref[pl.ds(start, 1024), :] = rows.T


def prepared(where, mine, other):
    return pl.pallas_call(
        prep_body,
        out_shape=jax.ShapeDtypeStruct((2048, 128), BF),
        in_specs=[pl.BlockSpec(memory_space=pltpu.SMEM)] + [pl.BlockSpec(memory_space=pltpu.VMEM)] * 2,
        cost_estimate=pl.CostEstimate(flops=500_000_000, bytes_accessed=1_000_000, transcendentals=0),
        name="prepared",
    )(where, mine, other)


def sums_body(leaf_ref, *refs):
    tiles, cols, out_ref = refs[:4], refs[4:8], refs[8]
    total = None
    for k_ref, s_ref in zip(tiles, cols):
        term = jnp.dot(k_ref[...], s_ref[...], preferred_element_type=F32)
        total = term if total is None else total + term

    @pl.when(pl.program_id(0) == 0)
    def _():
        out_ref[...] = total

    @pl.when(pl.program_id(0) != 0)
    def _():
        out_ref[...] += total


def leaf_sums(leaf, tiles, cols):
    step = 512
    return pl.pallas_call(
        sums_body,
        out_shape=jax.ShapeDtypeStruct((LEAF, 128), F32),
        grid_spec=pltpu.PrefetchScalarGridSpec(
            num_scalar_prefetch=1,
            grid=(2048 // step,),
            in_specs=[pl.BlockSpec((LEAF, step), lambda i, leaf: (leaf[0], i))] * 4
            + [pl.BlockSpec((step, 128), lambda i, leaf: (i, 0))] * 4,
            out_specs=pl.BlockSpec((LEAF, 128), lambda i, leaf: (0, 0)),
        ),
        cost_estimate=pl.CostEstimate(flops=3_000_000_000, bytes_accessed=9_000_000, transcendentals=0),
        name="leaf_sums",
    )(leaf, *tiles, *cols)


def eliminate(gram, aug_ref, top_ref):
    n = 128
    i = lax.broadcasted_iota(jnp.int32, (n, n), 0)
    j = lax.broadcasted_iota(jnp.int32, (n, n), 1)
    aug_ref[:, :n] = gram
    aug_ref[:, n:] = jnp.where(i == j, 1.0, 0.0)
    sub = lax.broadcasted_iota(jnp.int32, (8, n), 0)
    lane = lax.broadcasted_iota(jnp.int32, (8, n), 1)
    for b in range(n // 8):
        at = 8 * b
        left = aug_ref[at:at + 8, :n]
        right = aug_ref[at:at + 8, n:]
        cols = [jnp.broadcast_to(left[:, at + k:at + k + 1], (8, n)) for k in range(8)]
        scale = jnp.zeros((8, n), F32)
        for k in range(8):
            piv = jnp.broadcast_to(cols[k][k:k + 1, :], (8, n))
            inv = lax.rsqrt(piv)
            scale = jnp.where(sub == k, inv, scale)
            if k < 7:
                mult = jnp.where(sub > k, cols[k] * (inv * inv), 0.0)
                for q in range(k + 1, 8):
                    cols[q] = cols[q] - mult * jnp.broadcast_to(cols[q][k:k + 1, :], (8, n))
                left = left - mult * jnp.broadcast_to(left[k:k + 1, :], (8, n))
                right = right - mult * jnp.broadcast_to(right[k:k + 1, :], (8, n))
        left = jnp.where(lane >= sub + at, left * scale, 0.0)
        right = right * scale
        top_ref[at:at + 8, :n] = left
        top_ref[at:at + 8, n:] = right
        if b < n // 8 - 1:
            l1, l2, l3 = parts3(left)
            r1, r2, r3 = parts3(right)
            lhs = jnp.concatenate([l1, l1, l2, l1, l2, l3], axis=0).astype(BF)
            rl = jnp.concatenate([l1, l2, l1, l3, l2, l1], axis=0)
            rr = jnp.concatenate([r1, r2, r1, r3, r2, r1], axis=0)
            rhs = jnp.concatenate([rl, rr], axis=1).astype(BF)
            upd = lax.dot_general(lhs, rhs, (((0,), (0,)), ((), ())), preferred_element_type=F32)
            aug_ref[at + 8:, :] -= upd[at + 8:, :]


def regular(gram):
    i = lax.broadcasted_iota(jnp.int32, gram.shape, 0)
    j = lax.broadcasted_iota(jnp.int32, gram.shape, 1)
    diag = jnp.where(i == j, gram, 0.0)
    lam = (ridge / gram.shape[0]) * jnp.sum(jnp.sum(diag, axis=1, keepdims=True), axis=0, keepdims=True)
    return gram + jnp.where(i == j, lam, 0.0), lam


def tdot(a, b):
    return lax.dot_general(a, b, (((0,), (0,)), ((), ())), precision=HI, preferred_element_type=F32)


def ndot(a, b):
    return lax.dot_general(a, b, (((1,), (1,)), ((), ())), precision=HI, preferred_element_type=F32)


def mdot(a, b):
    return lax.dot_general(a, b, (((1,), (0,)), ((), ())), precision=HI, preferred_element_type=F32)


def leaf_body(a_ref, b_ref, c_ref, d_ref, z_ref, inv_ref, proj_ref, sq_ref, aug_ref, top_ref):
    z = (a_ref[...] + b_ref[...]) + (c_ref[...] + d_ref[...])
    z_ref[...] = z
    gram, lam = regular(tdot(z, z) * (1.0 / z.shape[0]))
    eliminate(gram, aug_ref, top_ref)
    inv = top_ref[:, 128:]
    proj = top_ref[:, :128] - lam * inv
    inv_ref[...] = inv
    proj_ref[...] = proj
    sq_ref[...] = tdot(proj, proj)


def node_body(a_ref, b_ref, inv_ref, proj_ref, sq_ref, aug_ref, top_ref):
    gram, lam = regular((a_ref[...] + b_ref[...]) * (1.0 / 256))
    eliminate(gram, aug_ref, top_ref)
    inv = top_ref[:, 128:]
    proj = top_ref[:, :128] - lam * inv
    inv_ref[...] = inv
    proj_ref[...] = proj
    sq_ref[...] = tdot(proj, proj)


def carry_body(z_ref, inv_ref, proj_ref, base_ref, next_ref):
    base = ndot(z_ref[...], inv_ref[...])
    base_ref[...] = base
    next_ref[...] = mdot(base, proj_ref[...])


def carry2_body(z_ref, inv_ref, proj_ref, next_ref):
    next_ref[...] = mdot(ndot(z_ref[...], inv_ref[...]), proj_ref[...])


def last_body(a_ref, b_ref, z_ref, out_ref, aug_ref, top_ref):
    gram, lam = regular((a_ref[...] + b_ref[...]) * (1.0 / 256))
    eliminate(gram, aug_ref, top_ref)
    out_ref[...] = ndot(z_ref[...], top_ref[:, 128:]) * (1.0 / 128)


def sds(*shape):
    return jax.ShapeDtypeStruct(shape, F32)


SCR = [pltpu.VMEM((128, 256), F32), pltpu.VMEM((128, 256), F32)]


def cost(f):
    return pl.CostEstimate(flops=f, bytes_accessed=400000, transcendentals=0)


def leaf_node(parts):
    outs = (sds(512, 128),) + (sds(128, 128),) * 3
    return pl.pallas_call(leaf_body, out_shape=outs, scratch_shapes=SCR, name="leaf_node")(*parts)


def pair_node(a, b):
    return pl.pallas_call(node_body, out_shape=(sds(128, 128),) * 3, scratch_shapes=SCR, name="pair_node")(a, b)


def carry(z, inv, proj):
    return pl.pallas_call(carry_body, out_shape=(sds(512, 128),) * 2, name="carry")(z, inv, proj)


def carry2(z, inv, proj):
    return pl.pallas_call(carry2_body, out_shape=sds(512, 128), name="carry2")(z, inv, proj)


def last_node(a, b, z):
    return pl.pallas_call(last_body, out_shape=sds(512, 128), scratch_shapes=SCR, name="last_node")(a, b, z)


ROW = ("z", "c")
COL = ("x", "y")


def moved(x, axis, by):
    size = lax.axis_size(axis)
    return lax.ppermute(x, axis, [(i, (i + by) % size) for i in range(size)])


def crossed(x, axis, bit):
    return lax.ppermute(x, axis, [(i, i ^ bit) for i in range(lax.axis_size(axis))])


def gathered_samples(samples, core):
    flat = samples.T
    half = flat.shape[1] // 2
    mine = lax.dynamic_slice_in_dim(flat, core * half, half, 1)
    away = lax.dynamic_slice_in_dim(flat, (1 - core) * half, half, 1)
    near = crossed(away, "c", 1)
    block = jnp.where(core == 0, jnp.concatenate([mine, near]), jnp.concatenate([near, mine]))[None]
    for bit in (1, 2, 4):
        block = jnp.concatenate([block, crossed(block, "z", bit)])
    blocks = [block] + [moved(block, "x", q) for q in (1, 2, 3)]
    return blocks, [crossed(b, "c", 1) for b in blocks]


def per_device(targets, sources, samples, near):
    z, core, x, y = (lax.axis_index(a) for a in ("z", "c", "x", "y"))
    pad = lambda v: jnp.pad(v, ((0, 5), (0, 0)))
    srcs = [sources] + [moved(sources, "x", q) for q in (1, 2, 3)]
    mine, other = gathered_samples(samples, core)
    tgt = pad(lax.dynamic_slice_in_dim(targets, x * 2048, 2048, 1))
    near_rows = lax.dynamic_slice_in_dim(near, x * 4, 4, 0)
    cols = (jnp.arange(16) // 4)
    from_x = jnp.mod(x - cols, 4)
    ids = (from_x * 4 + y) * 4 + jnp.arange(16) % 4
    hits = jnp.any(near_rows[:, :, None] == ids[None, None, :], axis=1)
    keep = jnp.where(hits, 0, 1).astype(jnp.int32)
    tiles = [kernel_tiles(keep[:, 4 * q:4 * q + 4], tgt, pad(srcs[q])) for q in range(4)]
    where = jnp.stack([z, core]).astype(jnp.int32)
    ready = [prepared(where, a, b) for a, b in zip(mine, other)]
    sums = {}
    for d in (2, 1, 3, 0):
        leaf = jnp.mod(y + d, 4).astype(jnp.int32).reshape(1)
        part = leaf_sums(leaf, tiles, ready)
        sums[d] = moved(part, "y", d) if d else part
    far_sample, inv0, proj0, sq0 = leaf_node([sums[d] for d in range(4)])
    sib = crossed(sq0, "y", 1)
    leaf_basis, carried = carry(far_sample, inv0, proj0)
    inv1, proj1, sq1 = pair_node(sq0, sib)
    cousin = crossed(sq1, "y", 2)
    carried = carry2(carried, inv1, proj1)
    nested = last_node(sq1, cousin, carried)
    return (leaf_basis, nested)


def solution(mesh):
    torus = Mesh(mesh.devices.reshape(8, 2, 4, 4), ("z", "c", "x", "y"))
    return jax.shard_map(
        per_device,
        mesh=torus,
        in_specs=(P(None, ROW), P(None, COL), P(COL, ROW), P(ROW, None)),
        out_specs=(P(ROW + COL, None), P(ROW + COL, None)),
        check_vma=False,
    )
```

```python
import functools

import jax
import jax.numpy as jnp
from jax import lax
from jax.sharding import Mesh
from jax.sharding import PartitionSpec as P
from jax.experimental import pallas as pl
from jax.experimental.pallas import tpu as pltpu

LEAF = 512
corr_length = 0.1
ridge = 0.1
LOG2E = 1.4426950408889634
HI = lax.Precision.HIGHEST
F32 = jnp.float32
BF = jnp.bfloat16


def parts3(x):
    a = x.astype(BF).astype(F32)
    rest = x - a
    b = rest.astype(BF).astype(F32)
    return a, b, rest - b


def features(pts_ref, centre, source, masked=0.0):
    points = pts_ref[...]
    row = lax.broadcasted_iota(jnp.int32, points.shape, 0)
    shift = jnp.where(row < 3, (points - centre) * (LOG2E / corr_length), 0.0)
    norm = jnp.sum(shift * shift, axis=0, keepdims=True) + masked
    if source:
        a, b, c = parts3(jnp.where(row == 3, norm, jnp.where(row == 4, 1.0, shift)))
        stack = [a, b, a, c, b, a]
    else:
        a, b, c = parts3(jnp.where(row == 4, norm, jnp.where(row == 3, 1.0, -2.0 * shift)))
        stack = [a, a, b, a, b, c]
    return jnp.concatenate(stack, axis=0).astype(BF)


def kernel_tile(rows, cols):
    d2 = lax.dot_general(rows, cols, (((0,), (0,)), ((), ())), preferred_element_type=F32)
    d2 = jnp.maximum(d2, 1e-24)
    return jnp.exp2(-(d2 * lax.rsqrt(d2))).astype(BF)


def target_features(tgt_ref, pts_ref, row_leaf):
    pts_ref[...] = jnp.zeros_like(pts_ref)
    pts_ref[0:3, :] = tgt_ref[:, pl.ds(pl.multiple_of(row_leaf * LEAF, LEAF), LEAF)]
    centre = jnp.mean(pts_ref[...], axis=1, keepdims=True)
    return features(pts_ref, centre, False), centre


def tile_of(q, i, leaf, at_ref, near_ref, src_ref, pts_ref, cols, centre):
    c, x, y = at_ref[1], at_ref[2], at_ref[3]
    chunk = jnp.bitwise_and(2 * c + i, 3)
    leaf_id = (jnp.bitwise_and(x - q, 3) * 4 + y) * 4 + chunk
    hit = near_ref[x * 4 + leaf, 0] == leaf_id
    for k in range(1, 8):
        hit = jnp.logical_or(hit, near_ref[x * 4 + leaf, k] == leaf_id)
    pts_ref[0:3, :] = src_ref[:, pl.ds(pl.multiple_of(chunk * LEAF, LEAF), LEAF)]
    return kernel_tile(features(pts_ref, centre, True, jnp.where(hit, 1e9, 0.0)), cols)


def tiles_body(q, at_ref, near_ref, tgt_ref, src_ref, out_ref, tpts_ref, spts_ref):
    leaf = pl.program_id(0)
    cols, centre = target_features(tgt_ref, tpts_ref, at_ref[2] * 4 + leaf)
    spts_ref[...] = jnp.zeros_like(spts_ref)
    for i in range(4):
        out_ref[i * LEAF:(i + 1) * LEAF, :] = tile_of(
            q, i, leaf, at_ref, near_ref, src_ref, spts_ref.at[i], cols, centre)


def kernel_tiles(q, at, near, targets, sources):
    return pl.pallas_call(
        functools.partial(tiles_body, q),
        out_shape=jax.ShapeDtypeStruct((2048, 2048), BF),
        grid_spec=pltpu.PrefetchScalarGridSpec(
            num_scalar_prefetch=2,
            grid=(4,),
            in_specs=[
                pl.BlockSpec((3, targets.shape[1]), lambda i, a, n: (0, 0)),
                pl.BlockSpec((3, 2048), lambda i, a, n: (0, 0)),
            ],
            out_specs=pl.BlockSpec((2048, LEAF), lambda i, a, n: (0, i)),
            scratch_shapes=[pltpu.VMEM((8, LEAF), F32), pltpu.VMEM((4, 8, LEAF), F32)],
        ),
        cost_estimate=pl.CostEstimate(flops=8_000_000_000, bytes_accessed=8_400_000, transcendentals=8_400_000),
        name="kernel_tiles",
    )(at, near, targets, sources)


def sums_body(turn, stored, fused, at_ref, near_ref, tgt_ref, *refs):
    ns, nf = len(stored), len(fused)
    tiles, refs = refs[:ns], refs[ns:]
    srcs, refs = refs[:nf], refs[nf:]
    mine, refs = refs[:ns + nf], refs[ns + nf:]
    other, refs = refs[:ns + nf], refs[ns + nf:]
    out_ref, tpts_ref, spts_ref = refs
    i = pl.program_id(0)
    leaf = jnp.bitwise_and(at_ref[3] + turn, 3)
    cols, centre = target_features(tgt_ref, tpts_ref, at_ref[2] * 4 + leaf)
    spts_ref[...] = jnp.zeros_like(spts_ref)
    total = jnp.zeros((128, LEAF), F32)
    for n in range(ns + nf):
        rows = jnp.where(i < 2, mine[n][...], other[n][...]).reshape(128, LEAF)
        if n < ns:
            tile = tiles[n][...]
        else:
            tile = tile_of(fused[n - ns], i, leaf, at_ref, near_ref, srcs[n - ns], spts_ref.at[n - ns], cols, centre)
        total += jnp.dot(rows, tile, preferred_element_type=F32)

    @pl.when(i == 0)
    def _():
        out_ref[...] = total

    @pl.when(i != 0)
    def _():
        out_ref[...] += total


def leaf_sums(turn, at, near, targets, tiles, sources, mine, other):
    stored, fused = sorted(tiles), sorted(sources)
    order = stored + fused
    width = len(fused)
    return pl.pallas_call(
        functools.partial(sums_body, turn, stored, fused),
        out_shape=jax.ShapeDtypeStruct((128, LEAF), F32),
        grid_spec=pltpu.PrefetchScalarGridSpec(
            num_scalar_prefetch=2,
            grid=(4,),
            in_specs=[pl.BlockSpec((3, targets.shape[1]), lambda i, a, n: (0, 0))]
            + [pl.BlockSpec((LEAF, LEAF), lambda i, a, n: (i, jnp.bitwise_and(a[3] + turn, 3)))] * len(stored)
            + [pl.BlockSpec((3, 2048), lambda i, a, n: (0, 0))] * width
            + [pl.BlockSpec((4, 32, LEAF), lambda i, a, n: (0, 0, jnp.minimum(i, 1)))] * 4
            + [pl.BlockSpec((4, 32, LEAF), lambda i, a, n: (0, 0, jnp.maximum(i - 2, 0)))] * 4,
            out_specs=pl.BlockSpec((128, LEAF), lambda i, a, n: (0, 0)),
            scratch_shapes=[pltpu.VMEM((8, LEAF), F32), pltpu.VMEM((width, 8, LEAF), F32)],
        ),
        cost_estimate=pl.CostEstimate(flops=4_000_000_000, bytes_accessed=9_000_000, transcendentals=1_000_000),
        name="leaf_sums",
    )(at, near, targets, *[tiles[q] for q in stored], *[sources[q] for q in fused],
      *[mine[q] for q in order], *[other[q] for q in order])


def eliminate(gram, aug_ref, top_ref):
    n = 128
    i = lax.broadcasted_iota(jnp.int32, (n, n), 0)
    j = lax.broadcasted_iota(jnp.int32, (n, n), 1)
    aug_ref[:, :n] = gram
    aug_ref[:, n:] = jnp.where(i == j, 1.0, 0.0)
    sub = lax.broadcasted_iota(jnp.int32, (8, n), 0)
    lane = lax.broadcasted_iota(jnp.int32, (8, n), 1)
    for b in range(n // 8):
        at = 8 * b
        left = aug_ref[at:at + 8, :n]
        right = aug_ref[at:at + 8, n:]
        cols = [jnp.broadcast_to(left[:, at + k:at + k + 1], (8, n)) for k in range(8)]
        scale = jnp.zeros((8, n), F32)
        for k in range(8):
            piv = jnp.broadcast_to(cols[k][k:k + 1, :], (8, n))
            inv = lax.rsqrt(piv)
            scale = jnp.where(sub == k, inv, scale)
            if k < 7:
                mult = jnp.where(sub > k, cols[k] * (inv * inv), 0.0)
                for q in range(k + 1, 8):
                    cols[q] = cols[q] - mult * jnp.broadcast_to(cols[q][k:k + 1, :], (8, n))
                left = left - mult * jnp.broadcast_to(left[k:k + 1, :], (8, n))
                right = right - mult * jnp.broadcast_to(right[k:k + 1, :], (8, n))
        left = jnp.where(lane >= sub + at, left * scale, 0.0)
        right = right * scale
        top_ref[at:at + 8, :n] = left
        top_ref[at:at + 8, n:] = right
        if b < n // 8 - 1:
            l1, l2, l3 = parts3(left)
            r1, r2, r3 = parts3(right)
            lhs = jnp.concatenate([l1, l1, l2, l1, l2, l3], axis=0).astype(BF)
            rl = jnp.concatenate([l1, l2, l1, l3, l2, l1], axis=0)
            rr = jnp.concatenate([r1, r2, r1, r3, r2, r1], axis=0)
            rhs = jnp.concatenate([rl, rr], axis=1).astype(BF)
            upd = lax.dot_general(lhs, rhs, (((0,), (0,)), ((), ())), preferred_element_type=F32)
            aug_ref[at + 8:, :] -= upd[at + 8:, :]


def regular(gram):
    i = lax.broadcasted_iota(jnp.int32, gram.shape, 0)
    j = lax.broadcasted_iota(jnp.int32, gram.shape, 1)
    diag = jnp.where(i == j, gram, 0.0)
    lam = (ridge / gram.shape[0]) * jnp.sum(jnp.sum(diag, axis=1, keepdims=True), axis=0, keepdims=True)
    return gram + jnp.where(i == j, lam, 0.0), lam


def tdot(a, b):
    return lax.dot_general(a, b, (((0,), (0,)), ((), ())), precision=HI, preferred_element_type=F32)


def ndot(a, b):
    return lax.dot_general(a, b, (((1,), (1,)), ((), ())), precision=HI, preferred_element_type=F32)


def mdot(a, b):
    return lax.dot_general(a, b, (((1,), (0,)), ((), ())), precision=HI, preferred_element_type=F32)


def leaf_body(at_ref, a_ref, b_ref, c_ref, d_ref, z_ref, inv_ref, proj_ref, sq_ref, aug_ref, top_ref):
    for k in range(4):
        for s in range(2):
            plane = jnp.bitwise_xor(jnp.bitwise_and(at_ref[0] - 2 * k, 7), s)
            rows = slice(16 * (2 * k + s), 16 * (2 * k + s) + 16)
            both = (a_ref[rows, :] + b_ref[rows, :]) + (c_ref[rows, :] + d_ref[rows, :])
            z_ref[pl.ds(pl.multiple_of(plane * 16, 16), 16), :] = both
    z = z_ref[...]
    gram, lam = regular(ndot(z, z) * (1.0 / LEAF))
    eliminate(gram, aug_ref, top_ref)
    inv = top_ref[:, 128:]
    proj = top_ref[:, :128] - lam * inv
    inv_ref[...] = inv
    proj_ref[...] = proj
    sq_ref[...] = tdot(proj, proj)


def node_body(a_ref, b_ref, inv_ref, proj_ref, sq_ref, aug_ref, top_ref):
    gram, lam = regular((a_ref[...] + b_ref[...]) * (1.0 / 256))
    eliminate(gram, aug_ref, top_ref)
    inv = top_ref[:, 128:]
    proj = top_ref[:, :128] - lam * inv
    inv_ref[...] = inv
    proj_ref[...] = proj
    sq_ref[...] = tdot(proj, proj)


def carry_body(z_ref, inv_ref, proj_ref, base_ref, next_ref):
    base = lax.dot_general(z_ref[...], inv_ref[...], (((0,), (1,)), ((), ())), precision=HI, preferred_element_type=F32)
    base_ref[...] = base
    next_ref[...] = mdot(base, proj_ref[...])


def carry2_body(z_ref, inv_ref, proj_ref, next_ref):
    next_ref[...] = mdot(ndot(z_ref[...], inv_ref[...]), proj_ref[...])


def last_body(a_ref, b_ref, z_ref, out_ref, aug_ref, top_ref):
    gram, lam = regular((a_ref[...] + b_ref[...]) * (1.0 / 256))
    eliminate(gram, aug_ref, top_ref)
    out_ref[...] = ndot(z_ref[...], top_ref[:, 128:]) * (1.0 / 128)


def sds(*shape):
    return jax.ShapeDtypeStruct(shape, F32)


SCR = [pltpu.VMEM((128, 256), F32), pltpu.VMEM((128, 256), F32)]


def cost(f):
    return pl.CostEstimate(flops=f, bytes_accessed=400000, transcendentals=0)


def leaf_node(at, parts):
    vm = pl.BlockSpec(memory_space=pltpu.VMEM)
    return pl.pallas_call(
        leaf_body,
        out_shape=(sds(128, LEAF),) + (sds(128, 128),) * 3,
        in_specs=[pl.BlockSpec(memory_space=pltpu.SMEM)] + [vm] * 4,
        scratch_shapes=SCR,
        name="leaf_node",
    )(at, *parts)


def pair_node(a, b):
    return pl.pallas_call(node_body, out_shape=(sds(128, 128),) * 3, scratch_shapes=SCR, name="pair_node")(a, b)


def carry(z, inv, proj):
    return pl.pallas_call(carry_body, out_shape=(sds(512, 128),) * 2, name="carry")(z, inv, proj)


def carry2(z, inv, proj):
    return pl.pallas_call(carry2_body, out_shape=sds(512, 128), name="carry2")(z, inv, proj)


def last_node(a, b, z):
    return pl.pallas_call(last_body, out_shape=sds(512, 128), scratch_shapes=SCR, name="last_node")(a, b, z)


ROW = ("z", "c")
COL = ("x", "y")


def moved(x, axis, by):
    size = lax.axis_size(axis)
    return lax.ppermute(x, axis, [(i, (i + by) % size) for i in range(size)])


def crossed(x, axis, bit):
    return lax.ppermute(x, axis, [(i, i ^ bit) for i in range(lax.axis_size(axis))])


def diagonal(x):
    return lax.ppermute(x, ROW, [(i, i ^ 3) for i in range(16)])


def own_half(samples, core):
    flat = samples.T
    half = flat.shape[1] // 2
    mine = lax.dynamic_slice_in_dim(flat, core * half, half, 1)
    away = lax.dynamic_slice_in_dim(flat, (1 - core) * half, half, 1)
    across, up, cross = crossed(away, "c", 1), crossed(mine, "z", 1), diagonal(away)
    first = jnp.where(core == 0, jnp.concatenate([mine, across]), jnp.concatenate([across, mine]))
    second = jnp.where(core == 0, jnp.concatenate([up, cross]), jnp.concatenate([cross, up]))
    pair = jnp.concatenate([first, second])
    return jnp.stack([pair] + [moved(pair, "z", 2 * k) for k in (1, 2, 3)])


def per_device(targets, sources, samples, near):
    at = jnp.stack([lax.axis_index(a) for a in ("z", "c", "x", "y")]).astype(jnp.int32)
    block = own_half(samples, at[1])
    srcs = [sources] + [moved(sources, "x", q) for q in (1, 2, 3)]
    mine = [block] + [moved(block, "x", q) for q in (1, 2, 3)]
    other = [crossed(b, "c", 1) for b in mine]
    stored = (0, 1, 3)
    tiles = {q: kernel_tiles(q, at, near, targets, srcs[q]) for q in stored}
    fused = {q: srcs[q] for q in range(4) if q not in stored}
    sums = {}
    for d in (2, 1, 3, 0):
        part = leaf_sums(d, at, near, targets, tiles, fused, mine, other)
        sums[d] = moved(part, "y", d) if d else part
    far_sample, inv0, proj0, sq0 = leaf_node(at, [sums[d] for d in range(4)])
    sib = crossed(sq0, "y", 1)
    leaf_basis, carried = carry(far_sample, inv0, proj0)
    inv1, proj1, sq1 = pair_node(sq0, sib)
    cousin = crossed(sq1, "y", 2)
    carried = carry2(carried, inv1, proj1)
    nested = last_node(sq1, cousin, carried)
    return (leaf_basis, nested)


def solution(mesh):
    torus = Mesh(mesh.devices.reshape(8, 2, 4, 4), ("z", "c", "x", "y"))
    return jax.shard_map(
        per_device,
        mesh=torus,
        in_specs=(P(None, ROW), P(None, COL), P(COL, ROW), P(ROW, None)),
        out_specs=(P(ROW + COL, None), P(ROW + COL, None)),
        check_vma=False,
    )
```

```python
import functools

import jax
import jax.numpy as jnp
from jax import lax
from jax.sharding import Mesh
from jax.sharding import PartitionSpec as P
from jax.experimental import pallas as pl
from jax.experimental.pallas import tpu as pltpu

LEAF = 512
corr_length = 0.1
ridge = 0.1
LOG2E = 1.4426950408889634
HI = lax.Precision.HIGHEST
F32 = jnp.float32
BF = jnp.bfloat16


def parts3(x):
    a = x.astype(BF).astype(F32)
    rest = x - a
    b = rest.astype(BF).astype(F32)
    return a, b, rest - b


def features(pts_ref, centre, source, masked=0.0):
    points = pts_ref[...]
    row = lax.broadcasted_iota(jnp.int32, points.shape, 0)
    shift = jnp.where(row < 3, (points - centre) * (LOG2E / corr_length), 0.0)
    norm = jnp.sum(shift * shift, axis=0, keepdims=True) + masked
    if source:
        a, b, c = parts3(jnp.where(row == 3, norm, jnp.where(row == 4, 1.0, shift)))
        stack = [a, b, a, c, b, a]
    else:
        a, b, c = parts3(jnp.where(row == 4, norm, jnp.where(row == 3, 1.0, -2.0 * shift)))
        stack = [a, a, b, a, b, c]
    return jnp.concatenate(stack, axis=0).astype(BF)


def kernel_tile(rows, cols):
    d2 = lax.dot_general(rows, cols, (((0,), (0,)), ((), ())), preferred_element_type=F32)
    d2 = jnp.maximum(d2, 1e-24)
    return jnp.exp2(-(d2 * lax.rsqrt(d2))).astype(BF)


def target_features(tgt_ref, pts_ref, row_leaf):
    pts_ref[...] = jnp.zeros_like(pts_ref)
    pts_ref[0:3, :] = tgt_ref[:, pl.ds(pl.multiple_of(row_leaf * LEAF, LEAF), LEAF)]
    centre = jnp.mean(pts_ref[...], axis=1, keepdims=True)
    return features(pts_ref, centre, False), centre


def tile_of(q, i, leaf, at_ref, near_ref, src_ref, pts_ref, cols, centre):
    c, x, y = at_ref[1], at_ref[2], at_ref[3]
    chunk = jnp.bitwise_and(2 * c + i, 3)
    leaf_id = (jnp.bitwise_and(x - q, 3) * 4 + y) * 4 + chunk
    hit = near_ref[x * 4 + leaf, 0] == leaf_id
    for k in range(1, 8):
        hit = jnp.logical_or(hit, near_ref[x * 4 + leaf, k] == leaf_id)
    pts_ref[0:3, :] = src_ref[:, pl.ds(pl.multiple_of(chunk * LEAF, LEAF), LEAF)]
    return kernel_tile(features(pts_ref, centre, True, jnp.where(hit, 1e9, 0.0)), cols)


def tiles_body(q, at_ref, near_ref, tgt_ref, src_ref, out_ref, tpts_ref, spts_ref):
    leaf = pl.program_id(0)
    cols, centre = target_features(tgt_ref, tpts_ref, at_ref[2] * 4 + leaf)
    spts_ref[...] = jnp.zeros_like(spts_ref)
    for i in range(4):
        out_ref[i * LEAF:(i + 1) * LEAF, :] = tile_of(
            q, i, leaf, at_ref, near_ref, src_ref, spts_ref.at[i], cols, centre)


def kernel_tiles(q, at, near, targets, sources):
    return pl.pallas_call(
        functools.partial(tiles_body, q),
        out_shape=jax.ShapeDtypeStruct((2048, 2048), BF),
        grid_spec=pltpu.PrefetchScalarGridSpec(
            num_scalar_prefetch=2,
            grid=(4,),
            in_specs=[
                pl.BlockSpec((3, targets.shape[1]), lambda i, a, n: (0, 0)),
                pl.BlockSpec((3, 2048), lambda i, a, n: (0, 0)),
            ],
            out_specs=pl.BlockSpec((2048, LEAF), lambda i, a, n: (0, i)),
            scratch_shapes=[pltpu.VMEM((8, LEAF), F32), pltpu.VMEM((4, 8, LEAF), F32)],
        ),
        cost_estimate=pl.CostEstimate(flops=8_000_000_000, bytes_accessed=8_400_000, transcendentals=8_400_000),
        name="kernel_tiles",
    )(at, near, targets, sources)


def sums_body(turn, stored, fused, at_ref, near_ref, tgt_ref, *refs):
    ns, nf = len(stored), len(fused)
    tiles, refs = refs[:ns], refs[ns:]
    srcs, refs = refs[:nf], refs[nf:]
    mine, refs = refs[:ns + nf], refs[ns + nf:]
    other, refs = refs[:ns + nf], refs[ns + nf:]
    out_ref, held_ref, tpts_ref, spts_ref, sems = refs
    leaf = jnp.bitwise_and(at_ref[3] + turn, 3)
    lanes = pl.ds(pl.multiple_of(leaf * LEAF, LEAF), LEAF)
    copies = [pltpu.make_async_copy(tiles[n].at[:, lanes], held_ref.at[n], sems.at[n]) for n in range(ns)]
    for copy in copies:
        copy.start()
    cols, centre = target_features(tgt_ref, tpts_ref, at_ref[2] * 4 + leaf)
    spts_ref[...] = jnp.zeros_like(spts_ref)
    for n in range(nf):
        for i in range(4):
            held_ref[ns + n, i * LEAF:(i + 1) * LEAF, :] = tile_of(
                fused[n], i, leaf, at_ref, near_ref, srcs[n], spts_ref.at[4 * n + i], cols, centre)
    for copy in copies:
        copy.wait()
    total = None
    for n in range(ns + nf):
        rows = jnp.concatenate([mine[n][...].reshape(128, 1024), other[n][...].reshape(128, 1024)], axis=1)
        term = jnp.dot(rows, held_ref[n], preferred_element_type=F32)
        total = term if total is None else total + term
    out_ref[...] = total


def leaf_sums(turn, at, near, targets, tiles, sources, mine, other):
    stored, fused = sorted(tiles), sorted(sources)
    order = stored + fused
    vm = pl.BlockSpec(memory_space=pltpu.VMEM)
    sm = pl.BlockSpec(memory_space=pltpu.SMEM)
    return pl.pallas_call(
        functools.partial(sums_body, turn, stored, fused),
        out_shape=jax.ShapeDtypeStruct((128, LEAF), F32),
        in_specs=[sm, sm, vm] + [pl.BlockSpec(memory_space=pl.ANY)] * len(stored) + [vm] * (len(fused) + 8),
        scratch_shapes=[
            pltpu.VMEM((4, 2048, LEAF), BF),
            pltpu.VMEM((8, LEAF), F32),
            pltpu.VMEM((4 * len(fused), 8, LEAF), F32),
            pltpu.SemaphoreType.DMA((len(stored),)),
        ],
        cost_estimate=pl.CostEstimate(flops=4_000_000_000, bytes_accessed=9_000_000, transcendentals=1_000_000),
        name="leaf_sums",
    )(at, near, targets, *[tiles[q] for q in stored], *[sources[q] for q in fused],
      *[mine[q] for q in order], *[other[q] for q in order])


def eliminate(gram, aug_ref, top_ref):
    n = 128
    i = lax.broadcasted_iota(jnp.int32, (n, n), 0)
    j = lax.broadcasted_iota(jnp.int32, (n, n), 1)
    aug_ref[:, :n] = gram
    aug_ref[:, n:] = jnp.where(i == j, 1.0, 0.0)
    sub = lax.broadcasted_iota(jnp.int32, (8, n), 0)
    lane = lax.broadcasted_iota(jnp.int32, (8, n), 1)
    for b in range(n // 8):
        at = 8 * b
        left = aug_ref[at:at + 8, :n]
        right = aug_ref[at:at + 8, n:]
        cols = [jnp.broadcast_to(left[:, at + k:at + k + 1], (8, n)) for k in range(8)]
        scale = jnp.zeros((8, n), F32)
        for k in range(8):
            piv = jnp.broadcast_to(cols[k][k:k + 1, :], (8, n))
            inv = lax.rsqrt(piv)
            scale = jnp.where(sub == k, inv, scale)
            if k < 7:
                mult = jnp.where(sub > k, cols[k] * (inv * inv), 0.0)
                for q in range(k + 1, 8):
                    cols[q] = cols[q] - mult * jnp.broadcast_to(cols[q][k:k + 1, :], (8, n))
                left = left - mult * jnp.broadcast_to(left[k:k + 1, :], (8, n))
                right = right - mult * jnp.broadcast_to(right[k:k + 1, :], (8, n))
        left = jnp.where(lane >= sub + at, left * scale, 0.0)
        right = right * scale
        top_ref[at:at + 8, :n] = left
        top_ref[at:at + 8, n:] = right
        if b < n // 8 - 1:
            l1, l2, l3 = parts3(left)
            r1, r2, r3 = parts3(right)
            lhs = jnp.concatenate([l1, l1, l2, l1, l2, l3], axis=0).astype(BF)
            rl = jnp.concatenate([l1, l2, l1, l3, l2, l1], axis=0)
            rr = jnp.concatenate([r1, r2, r1, r3, r2, r1], axis=0)
            rhs = jnp.concatenate([rl, rr], axis=1).astype(BF)
            upd = lax.dot_general(lhs, rhs, (((0,), (0,)), ((), ())), preferred_element_type=F32)
            aug_ref[at + 8:, :] -= upd[at + 8:, :]


def regular(gram):
    i = lax.broadcasted_iota(jnp.int32, gram.shape, 0)
    j = lax.broadcasted_iota(jnp.int32, gram.shape, 1)
    diag = jnp.where(i == j, gram, 0.0)
    lam = (ridge / gram.shape[0]) * jnp.sum(jnp.sum(diag, axis=1, keepdims=True), axis=0, keepdims=True)
    return gram + jnp.where(i == j, lam, 0.0), lam


def tdot(a, b):
    return lax.dot_general(a, b, (((0,), (0,)), ((), ())), precision=HI, preferred_element_type=F32)


def ndot(a, b):
    return lax.dot_general(a, b, (((1,), (1,)), ((), ())), precision=HI, preferred_element_type=F32)


def mdot(a, b):
    return lax.dot_general(a, b, (((1,), (0,)), ((), ())), precision=HI, preferred_element_type=F32)


def leaf_body(at_ref, a_ref, b_ref, c_ref, d_ref, z_ref, inv_ref, proj_ref, sq_ref, aug_ref, top_ref):
    for k in range(4):
        for s in range(2):
            plane = jnp.bitwise_xor(jnp.bitwise_and(at_ref[0] - 2 * k, 7), s)
            rows = slice(16 * (2 * k + s), 16 * (2 * k + s) + 16)
            both = (a_ref[rows, :] + b_ref[rows, :]) + (c_ref[rows, :] + d_ref[rows, :])
            z_ref[pl.ds(pl.multiple_of(plane * 16, 16), 16), :] = both
    z = z_ref[...]
    gram, lam = regular(ndot(z, z) * (1.0 / LEAF))
    eliminate(gram, aug_ref, top_ref)
    inv = top_ref[:, 128:]
    proj = top_ref[:, :128] - lam * inv
    inv_ref[...] = inv
    proj_ref[...] = proj
    sq_ref[...] = tdot(proj, proj)


def node_body(a_ref, b_ref, inv_ref, proj_ref, sq_ref, aug_ref, top_ref):
    gram, lam = regular((a_ref[...] + b_ref[...]) * (1.0 / 256))
    eliminate(gram, aug_ref, top_ref)
    inv = top_ref[:, 128:]
    proj = top_ref[:, :128] - lam * inv
    inv_ref[...] = inv
    proj_ref[...] = proj
    sq_ref[...] = tdot(proj, proj)


def carry_body(z_ref, inv_ref, proj_ref, base_ref, next_ref):
    base = lax.dot_general(z_ref[...], inv_ref[...], (((0,), (1,)), ((), ())), precision=HI, preferred_element_type=F32)
    base_ref[...] = base
    next_ref[...] = mdot(base, proj_ref[...])


def carry2_body(z_ref, inv_ref, proj_ref, next_ref):
    next_ref[...] = mdot(ndot(z_ref[...], inv_ref[...]), proj_ref[...])


def last_body(a_ref, b_ref, z_ref, out_ref, aug_ref, top_ref):
    gram, lam = regular((a_ref[...] + b_ref[...]) * (1.0 / 256))
    eliminate(gram, aug_ref, top_ref)
    out_ref[...] = ndot(z_ref[...], top_ref[:, 128:]) * (1.0 / 128)


def sds(*shape):
    return jax.ShapeDtypeStruct(shape, F32)


SCR = [pltpu.VMEM((128, 256), F32), pltpu.VMEM((128, 256), F32)]


def cost(f):
    return pl.CostEstimate(flops=f, bytes_accessed=400000, transcendentals=0)


def leaf_node(at, parts):
    vm = pl.BlockSpec(memory_space=pltpu.VMEM)
    return pl.pallas_call(
        leaf_body,
        out_shape=(sds(128, LEAF),) + (sds(128, 128),) * 3,
        in_specs=[pl.BlockSpec(memory_space=pltpu.SMEM)] + [vm] * 4,
        scratch_shapes=SCR,
        name="leaf_node",
    )(at, *parts)


def pair_node(a, b):
    return pl.pallas_call(node_body, out_shape=(sds(128, 128),) * 3, scratch_shapes=SCR, name="pair_node")(a, b)


def carry(z, inv, proj):
    return pl.pallas_call(carry_body, out_shape=(sds(512, 128),) * 2, name="carry")(z, inv, proj)


def carry2(z, inv, proj):
    return pl.pallas_call(carry2_body, out_shape=sds(512, 128), name="carry2")(z, inv, proj)


def last_node(a, b, z):
    return pl.pallas_call(last_body, out_shape=sds(512, 128), scratch_shapes=SCR, name="last_node")(a, b, z)


ROW = ("z", "c")
COL = ("x", "y")


def moved(x, axis, by):
    size = lax.axis_size(axis)
    return lax.ppermute(x, axis, [(i, (i + by) % size) for i in range(size)])


def crossed(x, axis, bit):
    return lax.ppermute(x, axis, [(i, i ^ bit) for i in range(lax.axis_size(axis))])


def diagonal(x):
    return lax.ppermute(x, ROW, [(i, i ^ 3) for i in range(16)])


def own_pair(samples, core):
    flat = samples.T
    half = flat.shape[1] // 2
    mine = lax.dynamic_slice_in_dim(flat, core * half, half, 1)
    away = lax.dynamic_slice_in_dim(flat, (1 - core) * half, half, 1)
    across, up, cross = crossed(away, "c", 1), crossed(mine, "z", 1), diagonal(away)
    first = jnp.where(core == 0, jnp.concatenate([mine, across]), jnp.concatenate([across, mine]))
    second = jnp.where(core == 0, jnp.concatenate([up, cross]), jnp.concatenate([cross, up]))
    return jnp.concatenate([first, second])


def after(x, *work):
    return lax.optimization_barrier((x, *work))[0]


def per_device(targets, sources, samples, near):
    at = jnp.stack([lax.axis_index(a) for a in ("z", "c", "x", "y")]).astype(jnp.int32)
    srcs = [sources] + [moved(sources, "x", q) for q in (1, 2, 3)]
    pair = own_pair(samples, at[1])
    tiles = {0: kernel_tiles(0, at, near, targets, sources)}
    pair = after(pair, tiles[0])
    block = jnp.stack([pair] + [moved(pair, "z", 2 * k) for k in (1, 2, 3)])
    tiles[1] = kernel_tiles(1, at, near, targets, srcs[1])
    block = after(block, tiles[1])
    mine = [block] + [moved(block, "x", q) for q in (1, 2, 3)]
    tiles[3] = kernel_tiles(3, at, near, targets, srcs[3])
    mine = [block] + [after(b, tiles[3]) for b in mine[1:]]
    other = [crossed(b, "c", 1) for b in mine]
    fused = {2: srcs[2]}
    sums = {}
    for d in (2, 1, 3, 0):
        part = leaf_sums(d, at, near, targets, tiles, fused, mine, other)
        sums[d] = moved(part, "y", d) if d else part
    far_sample, inv0, proj0, sq0 = leaf_node(at, [sums[d] for d in range(4)])
    sib = crossed(sq0, "y", 1)
    leaf_basis, carried = carry(far_sample, inv0, proj0)
    inv1, proj1, sq1 = pair_node(sq0, after(sib, carried))
    cousin = crossed(sq1, "y", 2)
    carried = carry2(carried, inv1, proj1)
    nested = last_node(sq1, cousin, carried)
    return (leaf_basis, nested)


def solution(mesh):
    torus = Mesh(mesh.devices.reshape(8, 2, 4, 4), ("z", "c", "x", "y"))
    return jax.shard_map(
        per_device,
        mesh=torus,
        in_specs=(P(None, ROW), P(None, COL), P(COL, ROW), P(ROW, None)),
        out_specs=(P(ROW + COL, None), P(ROW + COL, None)),
        check_vma=False,
    )
```

```python
import functools

import jax
import jax.numpy as jnp
from jax import lax
from jax.sharding import Mesh
from jax.sharding import PartitionSpec as P
from jax.experimental import pallas as pl
from jax.experimental.pallas import tpu as pltpu

LEAF = 512
corr_length = 0.1
ridge = 0.1
LOG2E = 1.4426950408889634
HI = lax.Precision.HIGHEST
F32 = jnp.float32
BF = jnp.bfloat16


def parts3(x):
    a = x.astype(BF).astype(F32)
    rest = x - a
    b = rest.astype(BF).astype(F32)
    return a, b, rest - b


def features(pts_ref, centre, source, masked=0.0):
    points = pts_ref[...]
    row = lax.broadcasted_iota(jnp.int32, points.shape, 0)
    shift = jnp.where(row < 3, (points - centre) * (LOG2E / corr_length), 0.0)
    norm = jnp.sum(shift * shift, axis=0, keepdims=True) + masked
    if source:
        a, b, c = parts3(jnp.where(row == 3, norm, jnp.where(row == 4, 1.0, shift)))
        stack = [a, b, a, c, b, a]
    else:
        a, b, c = parts3(jnp.where(row == 4, norm, jnp.where(row == 3, 1.0, -2.0 * shift)))
        stack = [a, a, b, a, b, c]
    return jnp.concatenate(stack, axis=0).astype(BF)


def kernel_tile(rows, cols):
    d2 = lax.dot_general(rows, cols, (((0,), (0,)), ((), ())), preferred_element_type=F32)
    d2 = jnp.maximum(d2, 1e-24)
    return jnp.exp2(-(d2 * lax.rsqrt(d2))).astype(BF)


def target_features(tgt_ref, pts_ref, row_leaf):
    pts_ref[...] = jnp.zeros_like(pts_ref)
    pts_ref[0:3, :] = tgt_ref[:, pl.ds(pl.multiple_of(row_leaf * LEAF, LEAF), LEAF)]
    centre = jnp.mean(pts_ref[...], axis=1, keepdims=True)
    return features(pts_ref, centre, False), centre


def place():
    return [lax.axis_index(a) for a in ("z", "c", "x", "y")]


def tile_of(q, i, leaf, near_ref, src_ref, pts_ref, cols, centre):
    _, c, x, y = place()
    chunk = jnp.bitwise_and(2 * c + i, 3)
    leaf_id = (jnp.bitwise_and(x - q, 3) * 4 + y) * 4 + chunk
    hit = near_ref[0, x * 4 + leaf] == leaf_id
    for k in range(1, 8):
        hit = jnp.logical_or(hit, near_ref[k, x * 4 + leaf] == leaf_id)
    pts_ref[0:3, :] = src_ref[:, pl.ds(pl.multiple_of(chunk * LEAF, LEAF), LEAF)]
    return kernel_tile(features(pts_ref, centre, True, jnp.where(hit, 1e9, 0.0)), cols)


def tiles_body(q, near_ref, tgt_ref, src_ref, out_ref, tpts_ref, spts_ref):
    _, _, x, y = place()
    spts_ref[...] = jnp.zeros_like(spts_ref)

    def one_leaf(turn, carry):
        leaf = jnp.bitwise_and(y + turn, 3)
        cols, centre = target_features(tgt_ref, tpts_ref, x * 4 + leaf)
        for i in range(4):
            out_ref[turn, i * LEAF:(i + 1) * LEAF, :] = tile_of(
                q, i, leaf, near_ref, src_ref, spts_ref.at[i], cols, centre)
        return carry

    lax.fori_loop(0, 4, one_leaf, 0)


def params():
    return pltpu.CompilerParams(vmem_limit_bytes=16 * 2**20)


def kernel_tiles(q, near, targets, sources):
    vm = pl.BlockSpec(memory_space=pltpu.VMEM)
    return pl.pallas_call(
        functools.partial(tiles_body, q),
        out_shape=jax.ShapeDtypeStruct((4, 2048, LEAF), BF),
        in_specs=[pl.BlockSpec(memory_space=pltpu.SMEM), vm, vm],
        out_specs=vm,
        scratch_shapes=[pltpu.VMEM((8, LEAF), F32), pltpu.VMEM((4, 8, LEAF), F32)],
        cost_estimate=pl.CostEstimate(flops=8_000_000_000, bytes_accessed=8_400_000, transcendentals=8_400_000),
        compiler_params=params(),
        name="kernel_tiles",
    )(near, targets, sources)


def sums_body(turn, stored, fused, near_ref, tgt_ref, *refs):
    ns, nf = len(stored), len(fused)
    tiles, refs = refs[:ns], refs[ns:]
    srcs, refs = refs[:nf], refs[nf:]
    mine, refs = refs[:ns + nf], refs[ns + nf:]
    other, refs = refs[:ns + nf], refs[ns + nf:]
    out_ref, held_ref, tpts_ref, spts_ref = refs
    _, _, x, y = place()
    leaf = jnp.bitwise_and(y + turn, 3)
    cols, centre = target_features(tgt_ref, tpts_ref, x * 4 + leaf)
    spts_ref[...] = jnp.zeros_like(spts_ref)
    total = None
    for n in range(ns + nf):
        rows = jnp.concatenate([mine[n][...].reshape(128, 1024), other[n][...].reshape(128, 1024)], axis=1)
        if n >= ns:
            for i in range(4):
                held_ref[n - ns, i * LEAF:(i + 1) * LEAF, :] = tile_of(
                    fused[n - ns], i, leaf, near_ref, srcs[n - ns], spts_ref.at[4 * (n - ns) + i], cols, centre)
            tile = held_ref[n - ns]
        else:
            tile = tiles[n][turn]
        term = jnp.dot(rows, tile, preferred_element_type=F32)
        total = term if total is None else total + term
    out_ref[...] = total


def leaf_sums(turn, near, targets, tiles, sources, mine, other):
    stored, fused = sorted(tiles), sorted(sources)
    order = stored + fused
    vm = pl.BlockSpec(memory_space=pltpu.VMEM)
    sm = pl.BlockSpec(memory_space=pltpu.SMEM)
    return pl.pallas_call(
        functools.partial(sums_body, turn, stored, fused),
        out_shape=jax.ShapeDtypeStruct((128, LEAF), F32),
        in_specs=[sm, vm] + [vm] * (len(stored) + len(fused) + 8),
        scratch_shapes=[
            pltpu.VMEM((len(fused), 2048, LEAF), BF),
            pltpu.VMEM((8, LEAF), F32),
            pltpu.VMEM((4 * len(fused), 8, LEAF), F32),
        ],
        cost_estimate=pl.CostEstimate(flops=4_000_000_000, bytes_accessed=9_000_000, transcendentals=1_000_000),
        compiler_params=params(),
        name="leaf_sums",
    )(near, targets, *[tiles[q] for q in stored], *[sources[q] for q in fused],
      *[mine[q] for q in order], *[other[q] for q in order])


def eliminate(gram, aug_ref, top_ref):
    n = 128
    i = lax.broadcasted_iota(jnp.int32, (n, n), 0)
    j = lax.broadcasted_iota(jnp.int32, (n, n), 1)
    aug_ref[:, :n] = gram
    aug_ref[:, n:] = jnp.where(i == j, 1.0, 0.0)
    sub = lax.broadcasted_iota(jnp.int32, (8, n), 0)
    lane = lax.broadcasted_iota(jnp.int32, (8, n), 1)
    for b in range(n // 8):
        at = 8 * b
        left = aug_ref[at:at + 8, :n]
        right = aug_ref[at:at + 8, n:]
        cols = [jnp.broadcast_to(left[:, at + k:at + k + 1], (8, n)) for k in range(8)]
        scale = jnp.zeros((8, n), F32)
        for k in range(8):
            piv = jnp.broadcast_to(cols[k][k:k + 1, :], (8, n))
            inv = lax.rsqrt(piv)
            scale = jnp.where(sub == k, inv, scale)
            if k < 7:
                mult = jnp.where(sub > k, cols[k] * (inv * inv), 0.0)
                for q in range(k + 1, 8):
                    cols[q] = cols[q] - mult * jnp.broadcast_to(cols[q][k:k + 1, :], (8, n))
                left = left - mult * jnp.broadcast_to(left[k:k + 1, :], (8, n))
                right = right - mult * jnp.broadcast_to(right[k:k + 1, :], (8, n))
        left = jnp.where(lane >= sub + at, left * scale, 0.0)
        right = right * scale
        top_ref[at:at + 8, :n] = left
        top_ref[at:at + 8, n:] = right
        if b < n // 8 - 1:
            l1, l2, l3 = parts3(left)
            r1, r2, r3 = parts3(right)
            lhs = jnp.concatenate([l1, l1, l2, l1, l2, l3], axis=0).astype(BF)
            rl = jnp.concatenate([l1, l2, l1, l3, l2, l1], axis=0)
            rr = jnp.concatenate([r1, r2, r1, r3, r2, r1], axis=0)
            rhs = jnp.concatenate([rl, rr], axis=1).astype(BF)
            upd = lax.dot_general(lhs, rhs, (((0,), (0,)), ((), ())), preferred_element_type=F32)
            aug_ref[at + 8:, :] -= upd[at + 8:, :]


def regular(gram):
    i = lax.broadcasted_iota(jnp.int32, gram.shape, 0)
    j = lax.broadcasted_iota(jnp.int32, gram.shape, 1)
    diag = jnp.where(i == j, gram, 0.0)
    lam = (ridge / gram.shape[0]) * jnp.sum(jnp.sum(diag, axis=1, keepdims=True), axis=0, keepdims=True)
    return gram + jnp.where(i == j, lam, 0.0), lam


def tdot(a, b):
    return lax.dot_general(a, b, (((0,), (0,)), ((), ())), precision=HI, preferred_element_type=F32)


def ndot(a, b):
    return lax.dot_general(a, b, (((1,), (1,)), ((), ())), precision=HI, preferred_element_type=F32)


def mdot(a, b):
    return lax.dot_general(a, b, (((1,), (0,)), ((), ())), precision=HI, preferred_element_type=F32)


def leaf_body(a_ref, b_ref, c_ref, d_ref, z_ref, inv_ref, proj_ref, sq_ref, aug_ref, top_ref):
    for k in range(4):
        for s in range(2):
            plane = jnp.bitwise_xor(jnp.bitwise_and(place()[0] - 2 * k, 7), s)
            rows = slice(16 * (2 * k + s), 16 * (2 * k + s) + 16)
            both = (a_ref[rows, :] + b_ref[rows, :]) + (c_ref[rows, :] + d_ref[rows, :])
            z_ref[pl.ds(pl.multiple_of(plane * 16, 16), 16), :] = both
    z = z_ref[...]
    gram, lam = regular(ndot(z, z) * (1.0 / LEAF))
    eliminate(gram, aug_ref, top_ref)
    inv = top_ref[:, 128:]
    proj = top_ref[:, :128] - lam * inv
    inv_ref[...] = inv
    proj_ref[...] = proj
    sq_ref[...] = tdot(proj, proj)


def node_body(a_ref, b_ref, inv_ref, proj_ref, sq_ref, aug_ref, top_ref):
    gram, lam = regular((a_ref[...] + b_ref[...]) * (1.0 / 256))
    eliminate(gram, aug_ref, top_ref)
    inv = top_ref[:, 128:]
    proj = top_ref[:, :128] - lam * inv
    inv_ref[...] = inv
    proj_ref[...] = proj
    sq_ref[...] = tdot(proj, proj)


def carry_body(z_ref, inv_ref, proj_ref, base_ref, next_ref):
    base = lax.dot_general(z_ref[...], inv_ref[...], (((0,), (1,)), ((), ())), precision=HI, preferred_element_type=F32)
    base_ref[...] = base
    next_ref[...] = mdot(base, proj_ref[...])


def carry2_body(z_ref, inv_ref, proj_ref, next_ref):
    next_ref[...] = mdot(ndot(z_ref[...], inv_ref[...]), proj_ref[...])


def last_body(a_ref, b_ref, z_ref, out_ref, aug_ref, top_ref):
    gram, lam = regular((a_ref[...] + b_ref[...]) * (1.0 / 256))
    eliminate(gram, aug_ref, top_ref)
    out_ref[...] = ndot(z_ref[...], top_ref[:, 128:]) * (1.0 / 128)


def sds(*shape):
    return jax.ShapeDtypeStruct(shape, F32)


SCR = [pltpu.VMEM((128, 256), F32), pltpu.VMEM((128, 256), F32)]


def cost(f):
    return pl.CostEstimate(flops=f, bytes_accessed=400000, transcendentals=0)


def leaf_node(parts):
    vm = pl.BlockSpec(memory_space=pltpu.VMEM)
    return pl.pallas_call(
        leaf_body,
        out_shape=(sds(128, LEAF),) + (sds(128, 128),) * 3,
        in_specs=[vm] * 4,
        scratch_shapes=SCR,
        name="leaf_node",
        compiler_params=params(),
    )(*parts)


def pair_node(a, b):
    return pl.pallas_call(node_body, out_shape=(sds(128, 128),) * 3, scratch_shapes=SCR, name="pair_node", compiler_params=params())(a, b)


def carry(z, inv, proj):
    return pl.pallas_call(carry_body, out_shape=(sds(512, 128),) * 2, name="carry", compiler_params=params())(z, inv, proj)


def carry2(z, inv, proj):
    return pl.pallas_call(carry2_body, out_shape=sds(512, 128), name="carry2", compiler_params=params())(z, inv, proj)


def last_node(a, b, z):
    return pl.pallas_call(last_body, out_shape=sds(512, 128), scratch_shapes=SCR, name="last_node", compiler_params=params())(a, b, z)


ROW = ("z", "c")
COL = ("x", "y")


def moved(x, axis, by):
    size = lax.axis_size(axis)
    return lax.ppermute(x, axis, [(i, (i + by) % size) for i in range(size)])


def crossed(x, axis, bit):
    return lax.ppermute(x, axis, [(i, i ^ bit) for i in range(lax.axis_size(axis))])


def diagonal(x):
    return lax.ppermute(x, ROW, [(i, i ^ 3) for i in range(16)])


def own_pair(samples, core):
    flat = samples.T
    half = flat.shape[1] // 2
    mine = lax.dynamic_slice_in_dim(flat, core * half, half, 1)
    away = lax.dynamic_slice_in_dim(flat, (1 - core) * half, half, 1)
    across, up, cross = crossed(away, "c", 1), crossed(mine, "z", 1), diagonal(away)
    first = jnp.where(core == 0, jnp.concatenate([mine, across]), jnp.concatenate([across, mine]))
    second = jnp.where(core == 0, jnp.concatenate([up, cross]), jnp.concatenate([cross, up]))
    return jnp.concatenate([first, second])


def after(x, *work):
    return lax.optimization_barrier((x, *work))[0]


def per_device(targets, sources, samples, near):
    core = lax.axis_index("c")
    near = near.T
    srcs = [sources] + [moved(sources, "x", q) for q in (1, 2, 3)]
    pair = own_pair(samples, core)
    tiles = {0: kernel_tiles(0, near, targets, sources)}
    pair = after(pair, tiles[0])
    block = jnp.stack([pair] + [moved(pair, "z", 2 * k) for k in (1, 2, 3)])
    tiles[1] = kernel_tiles(1, near, targets, after(srcs[1], srcs[2], srcs[3]))
    block = after(block, tiles[1])
    mine = [block] + [moved(block, "x", q) for q in (1, 2, 3)]
    tiles[3] = kernel_tiles(3, near, targets, srcs[3])
    mine = [block] + [after(b, tiles[3]) for b in mine[1:]]
    other = [crossed(b, "c", 1) for b in mine]
    fused = {2: srcs[2]}
    sums = {}
    for d in (2, 1, 3, 0):
        part = leaf_sums(d, near, targets, tiles, fused, mine, other)
        sums[d] = moved(part, "y", d) if d else part
    far_sample, inv0, proj0, sq0 = leaf_node([sums[d] for d in range(4)])
    sib = crossed(sq0, "y", 1)
    leaf_basis, carried = carry(far_sample, inv0, proj0)
    inv1, proj1, sq1 = pair_node(sq0, after(sib, carried))
    cousin = crossed(sq1, "y", 2)
    carried = carry2(carried, inv1, proj1)
    nested = last_node(sq1, cousin, carried)
    return (leaf_basis, nested)


def solution(mesh):
    torus = Mesh(mesh.devices.reshape(8, 2, 4, 4), ("z", "c", "x", "y"))
    return jax.shard_map(
        per_device,
        mesh=torus,
        in_specs=(P(None, ROW), P(None, COL), P(COL, ROW), P(ROW, None)),
        out_specs=(P(ROW + COL, None), P(ROW + COL, None)),
        check_vma=False,
    )
```

```python
import functools

import jax
import jax.numpy as jnp
from jax import lax
from jax.sharding import Mesh
from jax.sharding import PartitionSpec as P
from jax.experimental import pallas as pl
from jax.experimental.pallas import tpu as pltpu

LEAF = 512
corr_length = 0.1
ridge = 0.1
LOG2E = 1.4426950408889634
HI = lax.Precision.HIGHEST
F32 = jnp.float32
BF = jnp.bfloat16


def parts3(x):
    a = x.astype(BF).astype(F32)
    rest = x - a
    b = rest.astype(BF).astype(F32)
    return a, b, rest - b


def features(pts_ref, centre, source, masked=0.0):
    points = pts_ref[...]
    row = lax.broadcasted_iota(jnp.int32, points.shape, 0)
    shift = jnp.where(row < 3, (points - centre) * (LOG2E / corr_length), 0.0)
    norm = jnp.sum(shift * shift, axis=0, keepdims=True) + masked
    if source:
        a, b, c = parts3(jnp.where(row == 3, norm, jnp.where(row == 4, 1.0, shift)))
        stack = [a, b, a, c, b, a]
    else:
        a, b, c = parts3(jnp.where(row == 4, norm, jnp.where(row == 3, 1.0, -2.0 * shift)))
        stack = [a, a, b, a, b, c]
    return jnp.concatenate(stack, axis=0).astype(BF)


def kernel_tile(rows, cols):
    d2 = lax.dot_general(rows, cols, (((0,), (0,)), ((), ())), preferred_element_type=F32)
    d2 = jnp.maximum(d2, 1e-24)
    return jnp.exp2(-(d2 * lax.rsqrt(d2))).astype(BF)


def target_features(tgt_ref, pts_ref, row_leaf):
    pts_ref[...] = jnp.zeros_like(pts_ref)
    pts_ref[0:3, :] = tgt_ref[:, pl.ds(pl.multiple_of(row_leaf * LEAF, LEAF), LEAF)]
    centre = jnp.mean(pts_ref[...], axis=1, keepdims=True)
    return features(pts_ref, centre, False), centre


def place():
    return [lax.axis_index(a) for a in ("z", "c", "x", "y")]


def tile_of(q, i, leaf, near_ref, src_ref, pts_ref, cols, centre):
    _, c, x, y = place()
    chunk = jnp.bitwise_and(2 * c + i, 3)
    leaf_id = (jnp.bitwise_xor(x, q) * 4 + y) * 4 + chunk
    hit = near_ref[0, x * 4 + leaf] == leaf_id
    for k in range(1, 8):
        hit = jnp.logical_or(hit, near_ref[k, x * 4 + leaf] == leaf_id)
    pts_ref[0:3, :] = src_ref[:, pl.ds(pl.multiple_of(chunk * LEAF, LEAF), LEAF)]
    return kernel_tile(features(pts_ref, centre, True, jnp.where(hit, 1e9, 0.0)), cols)


def tiles_body(q, near_ref, tgt_ref, src_ref, out_ref, tpts_ref, spts_ref):
    _, _, x, y = place()
    spts_ref[...] = jnp.zeros_like(spts_ref)

    def one_leaf(turn, carry):
        leaf = jnp.bitwise_and(y + turn, 3)
        cols, centre = target_features(tgt_ref, tpts_ref, x * 4 + leaf)
        for i in range(4):
            out_ref[turn, i * LEAF:(i + 1) * LEAF, :] = tile_of(
                q, i, leaf, near_ref, src_ref, spts_ref.at[i], cols, centre)
        return carry

    lax.fori_loop(0, 4, one_leaf, 0)


def params():
    return pltpu.CompilerParams(vmem_limit_bytes=16 * 2**20)


def kernel_tiles(q, near, targets, sources):
    vm = pl.BlockSpec(memory_space=pltpu.VMEM)
    return pl.pallas_call(
        functools.partial(tiles_body, q),
        out_shape=jax.ShapeDtypeStruct((4, 2048, LEAF), BF),
        in_specs=[pl.BlockSpec(memory_space=pltpu.SMEM), vm, vm],
        out_specs=vm,
        scratch_shapes=[pltpu.VMEM((8, LEAF), F32), pltpu.VMEM((4, 8, LEAF), F32)],
        cost_estimate=pl.CostEstimate(flops=8_000_000_000, bytes_accessed=8_400_000, transcendentals=8_400_000),
        compiler_params=params(),
        name="kernel_tiles",
    )(near, targets, sources)


def own_body(near_ref, tgt_ref, src_ref, mine_ref, other_ref, out_ref, held_ref, tpts_ref, spts_ref):
    _, _, x, y = place()
    spts_ref[...] = jnp.zeros_like(spts_ref)

    def one_leaf(turn, carry):
        leaf = jnp.bitwise_and(y + turn, 3)
        cols, centre = target_features(tgt_ref, tpts_ref, x * 4 + leaf)
        total = None
        for n, rows_ref in enumerate((mine_ref, other_ref)):
            for i in (2 * n, 2 * n + 1):
                held_ref[i * LEAF:(i + 1) * LEAF, :] = tile_of(
                    0, i, leaf, near_ref, src_ref, spts_ref.at[i], cols, centre)
            term = jnp.dot(rows_ref[...].reshape(128, 1024), held_ref[1024 * n:1024 * (n + 1), :], preferred_element_type=F32)
            total = term if total is None else total + term
        out_ref[turn] = total
        return carry

    lax.fori_loop(0, 4, one_leaf, 0)


def own_sums(near, targets, sources, mine, other):
    vm = pl.BlockSpec(memory_space=pltpu.VMEM)
    return pl.pallas_call(
        own_body,
        out_shape=jax.ShapeDtypeStruct((4, 128, LEAF), F32),
        in_specs=[pl.BlockSpec(memory_space=pltpu.SMEM)] + [vm] * 4,
        out_specs=vm,
        scratch_shapes=[pltpu.VMEM((2048, LEAF), BF), pltpu.VMEM((8, LEAF), F32), pltpu.VMEM((4, 8, LEAF), F32)],
        cost_estimate=pl.CostEstimate(flops=8_000_000_000, bytes_accessed=8_400_000, transcendentals=8_400_000),
        compiler_params=params(),
        name="own_sums",
    )(near, targets, sources, mine, other)


def sums_body(turn, stored, fused, near_ref, tgt_ref, base_ref, *refs):
    ns, nf = len(stored), len(fused)
    tiles, refs = refs[:ns], refs[ns:]
    srcs, refs = refs[:nf], refs[nf:]
    mine, refs = refs[:ns + nf], refs[ns + nf:]
    other, refs = refs[:ns + nf], refs[ns + nf:]
    out_ref, held_ref, tpts_ref, spts_ref = refs
    _, _, x, y = place()
    leaf = jnp.bitwise_and(y + turn, 3)
    cols, centre = target_features(tgt_ref, tpts_ref, x * 4 + leaf)
    spts_ref[...] = jnp.zeros_like(spts_ref)
    total = base_ref[turn]
    for n in range(ns + nf):
        rows = jnp.concatenate([mine[n][...].reshape(128, 1024), other[n][...].reshape(128, 1024)], axis=1)
        if n >= ns:
            for i in range(4):
                held_ref[n - ns, i * LEAF:(i + 1) * LEAF, :] = tile_of(
                    fused[n - ns], i, leaf, near_ref, srcs[n - ns], spts_ref.at[4 * (n - ns) + i], cols, centre)
            tile = held_ref[n - ns]
        else:
            tile = tiles[n][turn]
        total = total + jnp.dot(rows, tile, preferred_element_type=F32)
    out_ref[...] = total


def leaf_sums(turn, near, targets, base, tiles, sources, mine, other):
    stored, fused = sorted(tiles), sorted(sources)
    order = stored + fused
    vm = pl.BlockSpec(memory_space=pltpu.VMEM)
    sm = pl.BlockSpec(memory_space=pltpu.SMEM)
    return pl.pallas_call(
        functools.partial(sums_body, turn, stored, fused),
        out_shape=jax.ShapeDtypeStruct((128, LEAF), F32),
        in_specs=[sm, vm, vm] + [vm] * (3 * (len(stored) + len(fused))),
        scratch_shapes=[
            pltpu.VMEM((len(fused), 2048, LEAF), BF),
            pltpu.VMEM((8, LEAF), F32),
            pltpu.VMEM((4 * len(fused), 8, LEAF), F32),
        ],
        cost_estimate=pl.CostEstimate(flops=4_000_000_000, bytes_accessed=9_000_000, transcendentals=1_000_000),
        compiler_params=params(),
        name="leaf_sums",
    )(near, targets, base, *[tiles[q] for q in stored], *[sources[q] for q in fused],
      *[mine[q] for q in order], *[other[q] for q in order])


def eliminate(gram, aug_ref, top_ref):
    n = 128
    i = lax.broadcasted_iota(jnp.int32, (n, n), 0)
    j = lax.broadcasted_iota(jnp.int32, (n, n), 1)
    aug_ref[:, :n] = gram
    aug_ref[:, n:] = jnp.where(i == j, 1.0, 0.0)
    sub = lax.broadcasted_iota(jnp.int32, (8, n), 0)
    lane = lax.broadcasted_iota(jnp.int32, (8, n), 1)
    for b in range(n // 8):
        at = 8 * b
        left = aug_ref[at:at + 8, :n]
        right = aug_ref[at:at + 8, n:]
        cols = [jnp.broadcast_to(left[:, at + k:at + k + 1], (8, n)) for k in range(8)]
        scale = jnp.zeros((8, n), F32)
        for k in range(8):
            piv = jnp.broadcast_to(cols[k][k:k + 1, :], (8, n))
            inv = lax.rsqrt(piv)
            scale = jnp.where(sub == k, inv, scale)
            if k < 7:
                mult = jnp.where(sub > k, cols[k] * (inv * inv), 0.0)
                for q in range(k + 1, 8):
                    cols[q] = cols[q] - mult * jnp.broadcast_to(cols[q][k:k + 1, :], (8, n))
                left = left - mult * jnp.broadcast_to(left[k:k + 1, :], (8, n))
                right = right - mult * jnp.broadcast_to(right[k:k + 1, :], (8, n))
        left = jnp.where(lane >= sub + at, left * scale, 0.0)
        right = right * scale
        top_ref[at:at + 8, :n] = left
        top_ref[at:at + 8, n:] = right
        if b < n // 8 - 1:
            l1, l2, l3 = parts3(left)
            r1, r2, r3 = parts3(right)
            lhs = jnp.concatenate([l1, l1, l2, l1, l2, l3], axis=0).astype(BF)
            rl = jnp.concatenate([l1, l2, l1, l3, l2, l1], axis=0)
            rr = jnp.concatenate([r1, r2, r1, r3, r2, r1], axis=0)
            rhs = jnp.concatenate([rl, rr], axis=1).astype(BF)
            upd = lax.dot_general(lhs, rhs, (((0,), (0,)), ((), ())), preferred_element_type=F32)
            aug_ref[at + 8:, :] -= upd[at + 8:, :]


def regular(gram):
    i = lax.broadcasted_iota(jnp.int32, gram.shape, 0)
    j = lax.broadcasted_iota(jnp.int32, gram.shape, 1)
    diag = jnp.where(i == j, gram, 0.0)
    lam = (ridge / gram.shape[0]) * jnp.sum(jnp.sum(diag, axis=1, keepdims=True), axis=0, keepdims=True)
    return gram + jnp.where(i == j, lam, 0.0), lam


def tdot(a, b):
    return lax.dot_general(a, b, (((0,), (0,)), ((), ())), precision=HI, preferred_element_type=F32)


def ndot(a, b):
    return lax.dot_general(a, b, (((1,), (1,)), ((), ())), precision=HI, preferred_element_type=F32)


def mdot(a, b):
    return lax.dot_general(a, b, (((1,), (0,)), ((), ())), precision=HI, preferred_element_type=F32)


def leaf_body(a_ref, b_ref, c_ref, d_ref, z_ref, inv_ref, proj_ref, sq_ref, aug_ref, top_ref):
    for k in range(4):
        for s in range(2):
            plane = jnp.bitwise_xor(jnp.bitwise_and(place()[0] - 2 * k, 7), s)
            rows = slice(16 * (2 * k + s), 16 * (2 * k + s) + 16)
            both = (a_ref[rows, :] + b_ref[rows, :]) + (c_ref[rows, :] + d_ref[rows, :])
            z_ref[pl.ds(pl.multiple_of(plane * 16, 16), 16), :] = both
    z = z_ref[...]
    gram, lam = regular(ndot(z, z) * (1.0 / LEAF))
    eliminate(gram, aug_ref, top_ref)
    inv = top_ref[:, 128:]
    proj = top_ref[:, :128] - lam * inv
    inv_ref[...] = inv
    proj_ref[...] = proj
    sq_ref[...] = tdot(proj, proj)


def node_body(a_ref, b_ref, inv_ref, proj_ref, sq_ref, aug_ref, top_ref):
    gram, lam = regular((a_ref[...] + b_ref[...]) * (1.0 / 256))
    eliminate(gram, aug_ref, top_ref)
    inv = top_ref[:, 128:]
    proj = top_ref[:, :128] - lam * inv
    inv_ref[...] = inv
    proj_ref[...] = proj
    sq_ref[...] = tdot(proj, proj)


def carry_body(z_ref, inv_ref, proj_ref, base_ref, next_ref):
    base = lax.dot_general(z_ref[...], inv_ref[...], (((0,), (1,)), ((), ())), precision=HI, preferred_element_type=F32)
    base_ref[...] = base
    next_ref[...] = mdot(base, proj_ref[...])


def carry2_body(z_ref, inv_ref, proj_ref, next_ref):
    next_ref[...] = mdot(ndot(z_ref[...], inv_ref[...]), proj_ref[...])


def last_body(a_ref, b_ref, z_ref, out_ref, aug_ref, top_ref):
    gram, lam = regular((a_ref[...] + b_ref[...]) * (1.0 / 256))
    eliminate(gram, aug_ref, top_ref)
    out_ref[...] = ndot(z_ref[...], top_ref[:, 128:]) * (1.0 / 128)


def sds(*shape):
    return jax.ShapeDtypeStruct(shape, F32)


SCR = [pltpu.VMEM((128, 256), F32), pltpu.VMEM((128, 256), F32)]


def cost(f):
    return pl.CostEstimate(flops=f, bytes_accessed=400000, transcendentals=0)


def leaf_node(parts):
    vm = pl.BlockSpec(memory_space=pltpu.VMEM)
    return pl.pallas_call(
        leaf_body,
        out_shape=(sds(128, LEAF),) + (sds(128, 128),) * 3,
        in_specs=[vm] * 4,
        scratch_shapes=SCR,
        name="leaf_node",
        compiler_params=params(),
    )(*parts)


def pair_node(a, b):
    return pl.pallas_call(node_body, out_shape=(sds(128, 128),) * 3, scratch_shapes=SCR, name="pair_node", compiler_params=params())(a, b)


def carry(z, inv, proj):
    return pl.pallas_call(carry_body, out_shape=(sds(512, 128),) * 2, name="carry", compiler_params=params())(z, inv, proj)


def carry2(z, inv, proj):
    return pl.pallas_call(carry2_body, out_shape=sds(512, 128), name="carry2", compiler_params=params())(z, inv, proj)


def last_node(a, b, z):
    return pl.pallas_call(last_body, out_shape=sds(512, 128), scratch_shapes=SCR, name="last_node", compiler_params=params())(a, b, z)


ROW = ("z", "c")
COL = ("x", "y")


def moved(x, axis, by):
    size = lax.axis_size(axis)
    return lax.ppermute(x, axis, [(i, (i + by) % size) for i in range(size)])


def crossed(x, axis, bit):
    return lax.ppermute(x, axis, [(i, i ^ bit) for i in range(lax.axis_size(axis))])


def diagonal(x):
    return lax.ppermute(x, ROW, [(i, i ^ 3) for i in range(16)])


def own_pair(samples, core):
    flat = samples.T
    half = flat.shape[1] // 2
    mine = lax.dynamic_slice_in_dim(flat, core * half, half, 1)
    away = lax.dynamic_slice_in_dim(flat, (1 - core) * half, half, 1)
    across, up, cross = crossed(away, "c", 1), crossed(mine, "z", 1), diagonal(away)
    first = jnp.where(core == 0, jnp.concatenate([mine, across]), jnp.concatenate([across, mine]))
    second = jnp.where(core == 0, jnp.concatenate([up, cross]), jnp.concatenate([cross, up]))
    return jnp.concatenate([first, second])


def after(x, *work):
    return lax.optimization_barrier((x, *work))[0]


def per_device(targets, sources, samples, near):
    core = lax.axis_index("c")
    near = near.T
    beside = crossed(sources, "x", 1)
    pair = own_pair(samples, core)
    block = jnp.stack([pair] + [moved(pair, "z", 2 * k) for k in (1, 2, 3)])
    behind = crossed(jnp.stack([sources, beside]), "x", 2)
    tiles = {1: kernel_tiles(1, near, targets, after(beside, pair))}
    block = after(block, tiles[1])
    sent = {q: crossed(block, "x", q) for q in (2, 1, 3)}
    swapped = crossed(block, "c", 1)
    tiles[3] = kernel_tiles(3, near, targets, after(behind[1], swapped))
    base = own_sums(near, targets, sources, block, after(swapped, tiles[3]))
    mine = {q: after(b, base) for q, b in sent.items()}
    other = {q: crossed(b, "c", 1) for q, b in mine.items()}
    fused = {2: behind[0]}
    sums = {}
    for d in (2, 1, 3, 0):
        part = leaf_sums(d, near, targets, base, tiles, fused, mine, other)
        sums[d] = moved(part, "y", d) if d else part
    far_sample, inv0, proj0, sq0 = leaf_node([sums[d] for d in range(4)])
    sib = crossed(sq0, "y", 1)
    leaf_basis, carried = carry(far_sample, inv0, proj0)
    inv1, proj1, sq1 = pair_node(sq0, after(sib, carried))
    cousin = crossed(sq1, "y", 2)
    carried = carry2(carried, inv1, proj1)
    nested = last_node(sq1, cousin, carried)
    return (leaf_basis, nested)


def solution(mesh):
    torus = Mesh(mesh.devices.reshape(8, 2, 4, 4), ("z", "c", "x", "y"))
    return jax.shard_map(
        per_device,
        mesh=torus,
        in_specs=(P(None, ROW), P(None, COL), P(COL, ROW), P(ROW, None)),
        out_specs=(P(ROW + COL, None), P(ROW + COL, None)),
        check_vma=False,
    )
```

```python
import functools

import jax
import jax.numpy as jnp
from jax import lax
from jax.sharding import Mesh
from jax.sharding import PartitionSpec as P
from jax.experimental import pallas as pl
from jax.experimental.pallas import tpu as pltpu


LEAF = 512
corr_length = 0.1
ridge = 0.1
LOG2E = 1.4426950408889634
HI = lax.Precision.HIGHEST
F32 = jnp.float32
BF = jnp.bfloat16


def parts3(x):
    a = x.astype(BF).astype(F32)
    rest = x - a
    b = rest.astype(BF).astype(F32)
    return a, b, rest - b


def features(pts_ref, centre, source, masked=0.0):
    points = pts_ref[...]
    row = lax.broadcasted_iota(jnp.int32, points.shape, 0)
    shift = jnp.where(row < 3, (points - centre) * (LOG2E / corr_length), 0.0)
    norm = jnp.sum(shift * shift, axis=0, keepdims=True) + masked
    if source:
        a, b, c = parts3(jnp.where(row == 3, norm, jnp.where(row == 4, 1.0, shift)))
        stack = [a, b, a, c, b, a]
    else:
        a, b, c = parts3(jnp.where(row == 4, norm, jnp.where(row == 3, 1.0, -2.0 * shift)))
        stack = [a, a, b, a, b, c]
    return jnp.concatenate(stack, axis=0).astype(BF)


def kernel_tile(rows, cols):
    d2 = lax.dot_general(rows, cols, (((0,), (0,)), ((), ())), preferred_element_type=F32)
    d2 = jnp.maximum(d2, 1e-24)
    return jnp.exp2(-(d2 * lax.rsqrt(d2))).astype(BF)


def target_features(tgt_ref, pts_ref, row_leaf):
    pts_ref[...] = jnp.zeros_like(pts_ref)
    pts_ref[0:3, :] = tgt_ref[:, pl.ds(pl.multiple_of(row_leaf * LEAF, LEAF), LEAF)]
    centre = jnp.mean(pts_ref[...], axis=1, keepdims=True)
    return features(pts_ref, centre, False), centre


def place():
    return [lax.axis_index(a) for a in ("z", "c", "x", "y")]


def tile_of(q, i, leaf, near_ref, src_ref, pts_ref, cols, centre):
    _, c, x, y = place()
    chunk = jnp.bitwise_and(2 * c + i, 3)
    leaf_id = (jnp.bitwise_xor(x, q) * 4 + y) * 4 + chunk
    hit = near_ref[0, x * 4 + leaf] == leaf_id
    for k in range(1, 8):
        hit = jnp.logical_or(hit, near_ref[k, x * 4 + leaf] == leaf_id)
    pts_ref[0:3, :] = src_ref[:, pl.ds(pl.multiple_of(chunk * LEAF, LEAF), LEAF)]
    return kernel_tile(features(pts_ref, centre, True, jnp.where(hit, 1e9, 0.0)), cols)


def tiles_body(q, first, near_ref, tgt_ref, src_ref, out_ref, tpts_ref, spts_ref):
    _, _, x, y = place()
    spts_ref[...] = jnp.zeros_like(spts_ref)

    def one_leaf(turn, carry):
        leaf = jnp.bitwise_and(y + turn, 3)
        cols, centre = target_features(tgt_ref, tpts_ref, x * 4 + leaf)
        for i in range(4):
            out_ref[turn - first, i * LEAF:(i + 1) * LEAF, :] = tile_of(
                q, i, leaf, near_ref, src_ref, spts_ref.at[i], cols, centre)
        return carry

    lax.fori_loop(first, 4, one_leaf, 0)


def params():
    return pltpu.CompilerParams(vmem_limit_bytes=16 * 2**20)


def kernel_tiles(q, first, near, targets, sources):
    vm = pl.BlockSpec(memory_space=pltpu.VMEM)
    return pl.pallas_call(
        functools.partial(tiles_body, q, first),
        out_shape=jax.ShapeDtypeStruct((4 - first, 2048, LEAF), BF),
        in_specs=[pl.BlockSpec(memory_space=pltpu.SMEM), vm, vm],
        out_specs=vm,
        scratch_shapes=[pltpu.VMEM((8, LEAF), F32), pltpu.VMEM((4, 8, LEAF), F32)],
        cost_estimate=pl.CostEstimate(flops=8_000_000_000, bytes_accessed=8_400_000, transcendentals=8_400_000),
        compiler_params=params(),
        name="kernel_tiles",
    )(near, targets, sources)


def own_body(near_ref, tgt_ref, src_ref, mine_ref, other_ref, out_ref, held_ref, tpts_ref, spts_ref):
    _, _, x, y = place()
    spts_ref[...] = jnp.zeros_like(spts_ref)

    def one_leaf(turn, carry):
        leaf = jnp.bitwise_and(y + turn, 3)
        cols, centre = target_features(tgt_ref, tpts_ref, x * 4 + leaf)
        total = None
        for n, rows_ref in enumerate((mine_ref, other_ref)):
            for i in (2 * n, 2 * n + 1):
                held_ref[i * LEAF:(i + 1) * LEAF, :] = tile_of(
                    0, i, leaf, near_ref, src_ref, spts_ref.at[i], cols, centre)
            term = jnp.dot(rows_ref[...].reshape(128, 1024), held_ref[1024 * n:1024 * (n + 1), :], preferred_element_type=F32)
            total = term if total is None else total + term
        out_ref[turn] = total
        return carry

    lax.fori_loop(0, 4, one_leaf, 0)


def own_sums(near, targets, sources, mine, other):
    vm = pl.BlockSpec(memory_space=pltpu.VMEM)
    return pl.pallas_call(
        own_body,
        out_shape=jax.ShapeDtypeStruct((4, 128, LEAF), F32),
        in_specs=[pl.BlockSpec(memory_space=pltpu.SMEM)] + [vm] * 4,
        out_specs=vm,
        scratch_shapes=[pltpu.VMEM((2048, LEAF), BF), pltpu.VMEM((8, LEAF), F32), pltpu.VMEM((4, 8, LEAF), F32)],
        cost_estimate=pl.CostEstimate(flops=8_000_000_000, bytes_accessed=8_400_000, transcendentals=8_400_000),
        compiler_params=params(),
        name="own_sums",
    )(near, targets, sources, mine, other)


def sums_body(turn, stored, fused, near_ref, tgt_ref, base_ref, *refs):
    ns, nf = len(stored), len(fused)
    tiles, refs = refs[:ns], refs[ns:]
    srcs, refs = refs[:nf], refs[nf:]
    mine, refs = refs[:ns + nf], refs[ns + nf:]
    other, refs = refs[:ns + nf], refs[ns + nf:]
    out_ref, held_ref, tpts_ref, spts_ref = refs
    _, _, x, y = place()
    leaf = jnp.bitwise_and(y + turn, 3)
    cols, centre = target_features(tgt_ref, tpts_ref, x * 4 + leaf)
    spts_ref[...] = jnp.zeros_like(spts_ref)
    total = base_ref[turn]
    for n in range(ns + nf):
        rows = jnp.concatenate([mine[n][...].reshape(128, 1024), other[n][...].reshape(128, 1024)], axis=1)
        if n >= ns:
            for i in range(4):
                held_ref[n - ns, i * LEAF:(i + 1) * LEAF, :] = tile_of(
                    fused[n - ns], i, leaf, near_ref, srcs[n - ns], spts_ref.at[4 * (n - ns) + i], cols, centre)
            tile = held_ref[n - ns]
        else:
            tile = tiles[n][turn - 4 + tiles[n].shape[0]]
        total = total + jnp.dot(rows, tile, preferred_element_type=F32)
    out_ref[...] = total


def leaf_sums(turn, near, targets, base, tiles, sources, mine, other):
    stored, fused = sorted(tiles), sorted(sources)
    order = stored + fused
    vm = pl.BlockSpec(memory_space=pltpu.VMEM)
    sm = pl.BlockSpec(memory_space=pltpu.SMEM)
    return pl.pallas_call(
        functools.partial(sums_body, turn, stored, fused),
        out_shape=jax.ShapeDtypeStruct((128, LEAF), F32),
        in_specs=[sm, vm, vm] + [vm] * (3 * (len(stored) + len(fused))),
        scratch_shapes=[
            pltpu.VMEM((len(fused), 2048, LEAF), BF),
            pltpu.VMEM((8, LEAF), F32),
            pltpu.VMEM((4 * len(fused), 8, LEAF), F32),
        ],
        cost_estimate=pl.CostEstimate(flops=4_000_000_000, bytes_accessed=9_000_000, transcendentals=1_000_000),
        compiler_params=params(),
        name="leaf_sums",
    )(near, targets, base, *[tiles[q] for q in stored], *[sources[q] for q in fused],
      *[mine[q] for q in order], *[other[q] for q in order])


def eliminate(gram, aug_ref, top_ref):
    n = 128
    i = lax.broadcasted_iota(jnp.int32, (n, n), 0)
    j = lax.broadcasted_iota(jnp.int32, (n, n), 1)
    aug_ref[:, :n] = gram
    aug_ref[:, n:] = jnp.where(i == j, 1.0, 0.0)
    sub = lax.broadcasted_iota(jnp.int32, (8, n), 0)
    lane = lax.broadcasted_iota(jnp.int32, (8, n), 1)
    for b in range(n // 8):
        at = 8 * b
        left = aug_ref[at:at + 8, :n]
        right = aug_ref[at:at + 8, n:]
        cols = [jnp.broadcast_to(left[:, at + k:at + k + 1], (8, n)) for k in range(8)]
        scale = jnp.zeros((8, n), F32)
        for k in range(0, 8, 2):
            a = jnp.broadcast_to(cols[k][k:k + 1, :], (8, n))
            off = jnp.broadcast_to(cols[k + 1][k:k + 1, :], (8, n))
            d = jnp.broadcast_to(cols[k + 1][k + 1:k + 2, :], (8, n))
            inv = lax.rsqrt(a)
            rest = lax.rsqrt(a * d - off * off)
            scale = jnp.where(sub == k, inv, jnp.where(sub == k + 1, (a * inv) * rest, scale))
            for j, square in ((k, inv * inv), (k + 1, a * (rest * rest))):
                if j < 7:
                    mult = jnp.where(sub > j, cols[j] * square, 0.0)
                    for q in range(j + 1, 8):
                        cols[q] = cols[q] - mult * jnp.broadcast_to(cols[q][j:j + 1, :], (8, n))
                    left = left - mult * jnp.broadcast_to(left[j:j + 1, :], (8, n))
                    right = right - mult * jnp.broadcast_to(right[j:j + 1, :], (8, n))
        left = jnp.where(lane >= sub + at, left * scale, 0.0)
        right = right * scale
        top_ref[at:at + 8, :n] = left
        top_ref[at:at + 8, n:] = right
        if b < n // 8 - 1:
            l1, l2, l3 = parts3(left)
            r1, r2, r3 = parts3(right)
            lhs = jnp.concatenate([l1, l1, l2, l1, l2, l3], axis=0).astype(BF)
            rl = jnp.concatenate([l1, l2, l1, l3, l2, l1], axis=0)
            rr = jnp.concatenate([r1, r2, r1, r3, r2, r1], axis=0)
            rhs = jnp.concatenate([rl, rr], axis=1).astype(BF)
            upd = lax.dot_general(lhs, rhs, (((0,), (0,)), ((), ())), preferred_element_type=F32)
            aug_ref[at + 8:, :] -= upd[at + 8:, :]


def regular(gram):
    i = lax.broadcasted_iota(jnp.int32, gram.shape, 0)
    j = lax.broadcasted_iota(jnp.int32, gram.shape, 1)
    diag = jnp.where(i == j, gram, 0.0)
    mean = jnp.sum(jnp.sum(diag, axis=1, keepdims=True), axis=0, keepdims=True) / gram.shape[0]
    return gram / mean + jnp.where(i == j, ridge, 0.0), mean


def factors(gram, aug_ref, top_ref):
    scaled, mean = regular(gram)
    eliminate(scaled, aug_ref, top_ref)
    inv = top_ref[:, 128:]
    root = lax.rsqrt(mean)
    return inv * root, (top_ref[:, :128] - ridge * inv) * (mean * root)


def tdot(a, b):
    return lax.dot_general(a, b, (((0,), (0,)), ((), ())), precision=HI, preferred_element_type=F32)


def ndot(a, b):
    return lax.dot_general(a, b, (((1,), (1,)), ((), ())), precision=HI, preferred_element_type=F32)


def mdot(a, b):
    return lax.dot_general(a, b, (((1,), (0,)), ((), ())), precision=HI, preferred_element_type=F32)


def leaf_body(a_ref, b_ref, c_ref, d_ref, z_ref, inv_ref, proj_ref, sq_ref, aug_ref, top_ref):
    for k in range(4):
        for s in range(2):
            plane = jnp.bitwise_xor(jnp.bitwise_and(place()[0] - 2 * k, 7), s)
            rows = slice(16 * (2 * k + s), 16 * (2 * k + s) + 16)
            both = (a_ref[rows, :] + b_ref[rows, :]) + (c_ref[rows, :] + d_ref[rows, :])
            z_ref[pl.ds(pl.multiple_of(plane * 16, 16), 16), :] = both
    z = z_ref[...]
    inv, proj = factors(ndot(z, z) * (1.0 / LEAF), aug_ref, top_ref)
    inv_ref[...] = inv
    proj_ref[...] = proj
    sq_ref[...] = tdot(proj, proj)


def node_body(a_ref, b_ref, inv_ref, proj_ref, sq_ref, aug_ref, top_ref):
    inv, proj = factors((a_ref[...] + b_ref[...]) * (1.0 / 256), aug_ref, top_ref)
    inv_ref[...] = inv
    proj_ref[...] = proj
    sq_ref[...] = tdot(proj, proj)


def carry_body(z_ref, inv_ref, proj_ref, base_ref, next_ref):
    base = lax.dot_general(z_ref[...], inv_ref[...], (((0,), (1,)), ((), ())), precision=HI, preferred_element_type=F32)
    base_ref[...] = base
    next_ref[...] = mdot(base, proj_ref[...])


def carry2_body(z_ref, inv_ref, proj_ref, next_ref):
    next_ref[...] = mdot(ndot(z_ref[...], inv_ref[...]), proj_ref[...])


def last_body(a_ref, b_ref, z_ref, out_ref, aug_ref, top_ref):
    inv, _ = factors((a_ref[...] + b_ref[...]) * (1.0 / 256), aug_ref, top_ref)
    out_ref[...] = ndot(z_ref[...], inv) * (1.0 / 128)


def sds(*shape):
    return jax.ShapeDtypeStruct(shape, F32)


SCR = [pltpu.VMEM((128, 256), F32), pltpu.VMEM((128, 256), F32)]


def leaf_node(parts):
    vm = pl.BlockSpec(memory_space=pltpu.VMEM)
    return pl.pallas_call(
        leaf_body,
        out_shape=(sds(128, LEAF),) + (sds(128, 128),) * 3,
        in_specs=[vm] * 4,
        scratch_shapes=SCR,
        name="leaf_node",
        compiler_params=params(),
    )(*parts)


def pair_node(a, b):
    return pl.pallas_call(node_body, out_shape=(sds(128, 128),) * 3, scratch_shapes=SCR, name="pair_node", compiler_params=params())(a, b)


def carry(z, inv, proj):
    return pl.pallas_call(carry_body, out_shape=(sds(512, 128),) * 2, name="carry", compiler_params=params())(z, inv, proj)


def carry2(z, inv, proj):
    return pl.pallas_call(carry2_body, out_shape=sds(512, 128), name="carry2", compiler_params=params())(z, inv, proj)


def last_node(a, b, z):
    return pl.pallas_call(last_body, out_shape=sds(512, 128), scratch_shapes=SCR, name="last_node", compiler_params=params())(a, b, z)


ROW = ("z", "c")
COL = ("x", "y")


def moved(x, axis, by):
    size = lax.axis_size(axis)
    return lax.ppermute(x, axis, [(i, (i + by) % size) for i in range(size)])


def crossed(x, axis, bit):
    return lax.ppermute(x, axis, [(i, i ^ bit) for i in range(lax.axis_size(axis))])


def diagonal(x):
    return lax.ppermute(x, ROW, [(i, i ^ 3) for i in range(16)])


def own_pair(samples, core):
    flat = samples.T
    half = flat.shape[1] // 2
    mine = lax.dynamic_slice_in_dim(flat, core * half, half, 1)
    away = lax.dynamic_slice_in_dim(flat, (1 - core) * half, half, 1)
    across, up, cross = crossed(away, "c", 1), crossed(mine, "z", 1), diagonal(away)
    first = jnp.where(core == 0, jnp.concatenate([mine, across]), jnp.concatenate([across, mine]))
    second = jnp.where(core == 0, jnp.concatenate([up, cross]), jnp.concatenate([cross, up]))
    return jnp.concatenate([first, second])


def after(x, *work):
    return lax.optimization_barrier((x, *work))[0]


def per_device(targets, sources, samples, near):
    core = lax.axis_index("c")
    near = near.T
    beside = crossed(sources, "x", 1)
    pair = own_pair(samples, core)
    block = jnp.stack([pair] + [moved(pair, "z", 2 * k) for k in (1, 2, 3)])
    behind = crossed(jnp.stack([sources, beside]), "x", 2)
    tiles = {1: kernel_tiles(1, 0, near, targets, after(beside, pair))}
    block = after(block, tiles[1])
    sent = {q: crossed(block, "x", q) for q in (2, 1, 3)}
    swapped = crossed(block, "c", 1)
    tiles[3] = kernel_tiles(3, 1, near, targets, after(behind[1], swapped))
    base = own_sums(near, targets, sources, block, after(swapped, tiles[3]))
    mine = {q: after(b, base) for q, b in sent.items()}
    other = {q: crossed(b, "c", 1) for q, b in mine.items()}
    sums = {}
    for d in (2, 1, 3, 0):
        made = tiles if d else {1: tiles[1]}
        fused = {2: behind[0]} if d else {2: behind[0], 3: behind[1]}
        part = leaf_sums(d, near, targets, base, made, fused, mine, other)
        sums[d] = moved(part, "y", d) if d else part
    far_sample, inv0, proj0, sq0 = leaf_node([sums[d] for d in range(4)])
    sib = crossed(sq0, "y", 1)
    leaf_basis, carried = carry(far_sample, inv0, proj0)
    inv1, proj1, sq1 = pair_node(sq0, after(sib, carried))
    cousin = crossed(sq1, "y", 2)
    carried = carry2(carried, inv1, proj1)
    nested = last_node(sq1, cousin, carried)
    return (leaf_basis, nested)


def solution(mesh):
    torus = Mesh(mesh.devices.reshape(8, 2, 4, 4), ("z", "c", "x", "y"))
    return jax.shard_map(
        per_device,
        mesh=torus,
        in_specs=(P(None, ROW), P(None, COL), P(COL, ROW), P(ROW, None)),
        out_specs=(P(ROW + COL, None), P(ROW + COL, None)),
        check_vma=False,
    )
```

```python
import functools

import jax
import jax.numpy as jnp
from jax import lax
from jax.sharding import Mesh
from jax.sharding import PartitionSpec as P
from jax.experimental import pallas as pl
from jax.experimental.pallas import tpu as pltpu


LEAF = 512
corr_length = 0.1
ridge = 0.1
LOG2E = 1.4426950408889634
HI = lax.Precision.HIGHEST
F32 = jnp.float32
BF = jnp.bfloat16


def parts3(x):
    a = x.astype(BF).astype(F32)
    rest = x - a
    b = rest.astype(BF).astype(F32)
    return a, b, rest - b


def features(pts_ref, centre, source, masked=0.0):
    points = pts_ref[...]
    row = lax.broadcasted_iota(jnp.int32, points.shape, 0)
    shift = jnp.where(row < 3, (points - centre) * (LOG2E / corr_length), 0.0)
    norm = jnp.sum(shift * shift, axis=0, keepdims=True) + masked
    if source:
        a, b, c = parts3(jnp.where(row == 3, norm, jnp.where(row == 4, 1.0, shift)))
        stack = [a, b, a, c, b, a]
    else:
        a, b, c = parts3(jnp.where(row == 4, norm, jnp.where(row == 3, 1.0, -2.0 * shift)))
        stack = [a, a, b, a, b, c]
    return jnp.concatenate(stack, axis=0).astype(BF)


def kernel_tile(rows, cols):
    d2 = lax.dot_general(rows, cols, (((0,), (0,)), ((), ())), preferred_element_type=F32)
    d2 = jnp.maximum(d2, 1e-24)
    return jnp.exp2(-(d2 * lax.rsqrt(d2))).astype(BF)


def target_features(tgt_ref, pts_ref, row_leaf):
    pts_ref[...] = jnp.zeros_like(pts_ref)
    pts_ref[0:3, :] = tgt_ref[:, pl.ds(pl.multiple_of(row_leaf * LEAF, LEAF), LEAF)]
    centre = jnp.mean(pts_ref[...], axis=1, keepdims=True)
    return features(pts_ref, centre, False), centre


def place():
    return [lax.axis_index(a) for a in ("z", "c", "x", "y")]


def tile_of(q, i, leaf, near_ref, src_ref, pts_ref, cols, centre):
    _, c, x, y = place()
    chunk = jnp.bitwise_and(2 * c + i, 3)
    leaf_id = (jnp.bitwise_xor(x, q) * 4 + y) * 4 + chunk
    hit = near_ref[0, x * 4 + leaf] == leaf_id
    for k in range(1, 8):
        hit = jnp.logical_or(hit, near_ref[k, x * 4 + leaf] == leaf_id)
    pts_ref[0:3, :] = src_ref[:, pl.ds(pl.multiple_of(chunk * LEAF, LEAF), LEAF)]
    return kernel_tile(features(pts_ref, centre, True, jnp.where(hit, 1e9, 0.0)), cols)


def tiles_body(q, first, near_ref, tgt_ref, src_ref, out_ref, tpts_ref, spts_ref):
    _, _, x, y = place()
    spts_ref[...] = jnp.zeros_like(spts_ref)

    def one_leaf(turn, carry):
        leaf = jnp.bitwise_and(y + turn, 3)
        cols, centre = target_features(tgt_ref, tpts_ref, x * 4 + leaf)
        for i in range(4):
            out_ref[turn - first, i * LEAF:(i + 1) * LEAF, :] = tile_of(
                q, i, leaf, near_ref, src_ref, spts_ref.at[i], cols, centre)
        return carry

    lax.fori_loop(first, 4, one_leaf, 0)


def params():
    return pltpu.CompilerParams(vmem_limit_bytes=16 * 2**20)


def kernel_tiles(q, first, near, targets, sources):
    vm = pl.BlockSpec(memory_space=pltpu.VMEM)
    return pl.pallas_call(
        functools.partial(tiles_body, q, first),
        out_shape=jax.ShapeDtypeStruct((4 - first, 2048, LEAF), BF),
        in_specs=[pl.BlockSpec(memory_space=pltpu.SMEM), vm, vm],
        out_specs=vm,
        scratch_shapes=[pltpu.VMEM((8, LEAF), F32), pltpu.VMEM((4, 8, LEAF), F32)],
        cost_estimate=pl.CostEstimate(flops=8_000_000_000, bytes_accessed=8_400_000, transcendentals=8_400_000),
        compiler_params=params(),
        name="kernel_tiles",
    )(near, targets, sources)


def own_body(near_ref, tgt_ref, src_ref, mine_ref, other_ref, out_ref, held_ref, tpts_ref, spts_ref):
    _, _, x, y = place()
    spts_ref[...] = jnp.zeros_like(spts_ref)

    def one_leaf(turn, carry):
        leaf = jnp.bitwise_and(y + turn, 3)
        cols, centre = target_features(tgt_ref, tpts_ref, x * 4 + leaf)
        total = None
        for n, rows_ref in enumerate((mine_ref, other_ref)):
            for i in (2 * n, 2 * n + 1):
                held_ref[i * LEAF:(i + 1) * LEAF, :] = tile_of(
                    0, i, leaf, near_ref, src_ref, spts_ref.at[i], cols, centre)
            term = jnp.dot(rows_ref[...].reshape(128, 1024), held_ref[1024 * n:1024 * (n + 1), :], preferred_element_type=F32)
            total = term if total is None else total + term
        out_ref[turn] = total
        return carry

    lax.fori_loop(0, 4, one_leaf, 0)


def own_sums(near, targets, sources, mine, other):
    vm = pl.BlockSpec(memory_space=pltpu.VMEM)
    return pl.pallas_call(
        own_body,
        out_shape=jax.ShapeDtypeStruct((4, 128, LEAF), F32),
        in_specs=[pl.BlockSpec(memory_space=pltpu.SMEM)] + [vm] * 4,
        out_specs=vm,
        scratch_shapes=[pltpu.VMEM((2048, LEAF), BF), pltpu.VMEM((8, LEAF), F32), pltpu.VMEM((4, 8, LEAF), F32)],
        cost_estimate=pl.CostEstimate(flops=8_000_000_000, bytes_accessed=8_400_000, transcendentals=8_400_000),
        compiler_params=params(),
        name="own_sums",
    )(near, targets, sources, mine, other)


def sums_body(turn, stored, fused, near_ref, tgt_ref, base_ref, *refs):
    ns, nf = len(stored), len(fused)
    tiles, refs = refs[:ns], refs[ns:]
    srcs, refs = refs[:nf], refs[nf:]
    mine, refs = refs[:ns + nf], refs[ns + nf:]
    other, refs = refs[:ns + nf], refs[ns + nf:]
    out_ref, held_ref, tpts_ref, spts_ref = refs
    _, _, x, y = place()
    leaf = jnp.bitwise_and(y + turn, 3)
    cols, centre = target_features(tgt_ref, tpts_ref, x * 4 + leaf)
    spts_ref[...] = jnp.zeros_like(spts_ref)
    total = base_ref[turn]
    for n in range(ns + nf):
        rows = jnp.concatenate([mine[n][...].reshape(128, 1024), other[n][...].reshape(128, 1024)], axis=1)
        if n >= ns:
            for i in range(4):
                held_ref[n - ns, i * LEAF:(i + 1) * LEAF, :] = tile_of(
                    fused[n - ns], i, leaf, near_ref, srcs[n - ns], spts_ref.at[4 * (n - ns) + i], cols, centre)
            tile = held_ref[n - ns]
        else:
            tile = tiles[n][turn - 4 + tiles[n].shape[0]]
        total = total + jnp.dot(rows, tile, preferred_element_type=F32)
    out_ref[...] = total


def leaf_sums(turn, near, targets, base, tiles, sources, mine, other):
    stored, fused = sorted(tiles), sorted(sources)
    order = stored + fused
    vm = pl.BlockSpec(memory_space=pltpu.VMEM)
    sm = pl.BlockSpec(memory_space=pltpu.SMEM)
    return pl.pallas_call(
        functools.partial(sums_body, turn, stored, fused),
        out_shape=jax.ShapeDtypeStruct((128, LEAF), F32),
        in_specs=[sm, vm, vm] + [vm] * (3 * (len(stored) + len(fused))),
        scratch_shapes=[
            pltpu.VMEM((len(fused), 2048, LEAF), BF),
            pltpu.VMEM((8, LEAF), F32),
            pltpu.VMEM((4 * len(fused), 8, LEAF), F32),
        ],
        cost_estimate=pl.CostEstimate(flops=4_000_000_000, bytes_accessed=9_000_000, transcendentals=1_000_000),
        compiler_params=params(),
        name="leaf_sums",
    )(near, targets, base, *[tiles[q] for q in stored], *[sources[q] for q in fused],
      *[mine[q] for q in order], *[other[q] for q in order])


def spread(x, lane):
    return jnp.take_along_axis(x, jnp.full(x.shape, lane, jnp.int32), axis=1, mode="promise_in_bounds")


def row(x, k):
    return jnp.broadcast_to(x[k:k + 1, :], x.shape)


def pivots(cols, k):
    a, off, d = row(cols[k], k), row(cols[k], k + 1), row(cols[k + 1], k + 1)
    inv = lax.rsqrt(a)
    rest = lax.rsqrt(a * d - off * off)
    return (inv, (a * inv) * rest), (inv * inv, a * (rest * rest))


def eliminate(gram, aug_ref, top_ref):
    n = 128
    i = lax.broadcasted_iota(jnp.int32, (n, n), 0)
    j = lax.broadcasted_iota(jnp.int32, (n, n), 1)
    aug_ref[:, :n] = gram
    aug_ref[:, n:] = jnp.where(i == j, 1.0, 0.0)
    sub = lax.broadcasted_iota(jnp.int32, (8, n), 0)
    lane = lax.broadcasted_iota(jnp.int32, (8, n), 1)
    for at in range(0, n, 16):
        high = [aug_ref[at:at + 8, :n], aug_ref[at:at + 8, n:]]
        low = [aug_ref[at + 8:at + 16, :n], aug_ref[at + 8:at + 16, n:]]
        upper = [spread(high[0], at + k) for k in range(8)]
        under = [spread(low[0], at + k) for k in range(8)]
        lower = [spread(low[0], at + 8 + k) for k in range(8)]
        scale_high = scale_low = jnp.zeros((8, n), F32)
        for k in range(0, 8, 2):
            scales, squares = pivots(upper, k)
            scale_high = jnp.where(sub == k, scales[0], jnp.where(sub == k + 1, scales[1], scale_high))
            for p, square in ((k, squares[0]), (k + 1, squares[1])):
                mult = jnp.where(sub > p, upper[p] * square, 0.0)
                wide = under[p] * square
                for q in range(p + 1, 8):
                    entry = row(upper[p], q)
                    upper[q] = upper[q] - mult * entry
                    under[q] = under[q] - wide * entry
                for q in range(8):
                    lower[q] = lower[q] - wide * row(under[p], q)
                for h in range(2):
                    line = row(high[h], p)
                    low[h] = low[h] - wide * line
                    if p < 7:
                        high[h] = high[h] - mult * line
        for k in range(0, 8, 2):
            scales, squares = pivots(lower, k)
            scale_low = jnp.where(sub == k, scales[0], jnp.where(sub == k + 1, scales[1], scale_low))
            for p, square in ((k, squares[0]), (k + 1, squares[1])):
                if p < 7:
                    mult = jnp.where(sub > p, lower[p] * square, 0.0)
                    for q in range(p + 1, 8):
                        lower[q] = lower[q] - mult * row(lower[p], q)
                    for h in range(2):
                        low[h] = low[h] - mult * row(low[h], p)
        left = [jnp.where(lane >= sub + at, high[0] * scale_high, 0.0), jnp.where(lane >= sub + at + 8, low[0] * scale_low, 0.0)]
        right = [high[1] * scale_high, low[1] * scale_low]
        for h in range(2):
            top_ref[at + 8 * h:at + 8 * h + 8, :n] = left[h]
            top_ref[at + 8 * h:at + 8 * h + 8, n:] = right[h]
        if at < n - 16:
            l1, l2, l3 = parts3(jnp.concatenate(left, axis=0))
            r1, r2, r3 = parts3(jnp.concatenate(right, axis=0))
            lhs = jnp.concatenate([l1, l1, l2, l1, l2, l3], axis=0).astype(BF)
            rl = jnp.concatenate([l1, l2, l1, l3, l2, l1], axis=0)
            rr = jnp.concatenate([r1, r2, r1, r3, r2, r1], axis=0)
            rhs = jnp.concatenate([rl, rr], axis=1).astype(BF)
            upd = lax.dot_general(lhs, rhs, (((0,), (0,)), ((), ())), preferred_element_type=F32)
            aug_ref[at + 16:, :] -= upd[at + 16:, :]


def regular(gram):
    i = lax.broadcasted_iota(jnp.int32, gram.shape, 0)
    j = lax.broadcasted_iota(jnp.int32, gram.shape, 1)
    diag = jnp.where(i == j, gram, 0.0)
    mean = jnp.sum(jnp.sum(diag, axis=1, keepdims=True), axis=0, keepdims=True) / gram.shape[0]
    return gram / mean + jnp.where(i == j, ridge, 0.0), mean


def factors(gram, aug_ref, top_ref):
    scaled, mean = regular(gram)
    eliminate(scaled, aug_ref, top_ref)
    inv = top_ref[:, 128:]
    root = lax.rsqrt(mean)
    return inv * root, (top_ref[:, :128] - ridge * inv) * (mean * root)


def tdot(a, b):
    return lax.dot_general(a, b, (((0,), (0,)), ((), ())), precision=HI, preferred_element_type=F32)


def ndot(a, b):
    return lax.dot_general(a, b, (((1,), (1,)), ((), ())), precision=HI, preferred_element_type=F32)


def mdot(a, b):
    return lax.dot_general(a, b, (((1,), (0,)), ((), ())), precision=HI, preferred_element_type=F32)


def leaf_body(a_ref, b_ref, c_ref, d_ref, z_ref, inv_ref, proj_ref, sq_ref, aug_ref, top_ref):
    for k in range(4):
        for s in range(2):
            plane = jnp.bitwise_xor(jnp.bitwise_and(place()[0] - 2 * k, 7), s)
            rows = slice(16 * (2 * k + s), 16 * (2 * k + s) + 16)
            both = (a_ref[rows, :] + b_ref[rows, :]) + (c_ref[rows, :] + d_ref[rows, :])
            z_ref[pl.ds(pl.multiple_of(plane * 16, 16), 16), :] = both
    z = z_ref[...]
    inv, proj = factors(ndot(z, z) * (1.0 / LEAF), aug_ref, top_ref)
    inv_ref[...] = inv
    proj_ref[...] = proj
    sq_ref[...] = tdot(proj, proj)


def node_body(a_ref, b_ref, inv_ref, proj_ref, sq_ref, aug_ref, top_ref):
    inv, proj = factors((a_ref[...] + b_ref[...]) * (1.0 / 256), aug_ref, top_ref)
    inv_ref[...] = inv
    proj_ref[...] = proj
    sq_ref[...] = tdot(proj, proj)


def carry_body(z_ref, inv_ref, proj_ref, base_ref, next_ref):
    base = lax.dot_general(z_ref[...], inv_ref[...], (((0,), (1,)), ((), ())), precision=HI, preferred_element_type=F32)
    base_ref[...] = base
    next_ref[...] = mdot(base, proj_ref[...])


def carry2_body(z_ref, inv_ref, proj_ref, next_ref):
    next_ref[...] = mdot(ndot(z_ref[...], inv_ref[...]), proj_ref[...])


def last_body(a_ref, b_ref, z_ref, out_ref, aug_ref, top_ref):
    inv, _ = factors((a_ref[...] + b_ref[...]) * (1.0 / 256), aug_ref, top_ref)
    out_ref[...] = ndot(z_ref[...], inv) * (1.0 / 128)


def sds(*shape):
    return jax.ShapeDtypeStruct(shape, F32)


SCR = [pltpu.VMEM((128, 256), F32), pltpu.VMEM((128, 256), F32)]


def leaf_node(parts):
    vm = pl.BlockSpec(memory_space=pltpu.VMEM)
    return pl.pallas_call(
        leaf_body,
        out_shape=(sds(128, LEAF),) + (sds(128, 128),) * 3,
        in_specs=[vm] * 4,
        scratch_shapes=SCR,
        name="leaf_node",
        compiler_params=params(),
    )(*parts)


def pair_node(a, b):
    return pl.pallas_call(node_body, out_shape=(sds(128, 128),) * 3, scratch_shapes=SCR, name="pair_node", compiler_params=params())(a, b)


def carry(z, inv, proj):
    return pl.pallas_call(carry_body, out_shape=(sds(512, 128),) * 2, name="carry", compiler_params=params())(z, inv, proj)


def carry2(z, inv, proj):
    return pl.pallas_call(carry2_body, out_shape=sds(512, 128), name="carry2", compiler_params=params())(z, inv, proj)


def last_node(a, b, z):
    return pl.pallas_call(last_body, out_shape=sds(512, 128), scratch_shapes=SCR, name="last_node", compiler_params=params())(a, b, z)


ROW = ("z", "c")
COL = ("x", "y")


def moved(x, axis, by):
    size = lax.axis_size(axis)
    return lax.ppermute(x, axis, [(i, (i + by) % size) for i in range(size)])


def crossed(x, axis, bit):
    return lax.ppermute(x, axis, [(i, i ^ bit) for i in range(lax.axis_size(axis))])


def diagonal(x):
    return lax.ppermute(x, ROW, [(i, i ^ 3) for i in range(16)])


def own_pair(samples, core):
    flat = samples.T
    half = flat.shape[1] // 2
    mine = lax.dynamic_slice_in_dim(flat, core * half, half, 1)
    away = lax.dynamic_slice_in_dim(flat, (1 - core) * half, half, 1)
    across, up, cross = crossed(away, "c", 1), crossed(mine, "z", 1), diagonal(away)
    first = jnp.where(core == 0, jnp.concatenate([mine, across]), jnp.concatenate([across, mine]))
    second = jnp.where(core == 0, jnp.concatenate([up, cross]), jnp.concatenate([cross, up]))
    return jnp.concatenate([first, second])


def after(x, *work):
    return lax.optimization_barrier((x, *work))[0]


def per_device(targets, sources, samples, near):
    core = lax.axis_index("c")
    near = near.T
    beside = crossed(sources, "x", 1)
    pair = own_pair(samples, core)
    block = jnp.stack([pair] + [moved(pair, "z", 2 * k) for k in (1, 2, 3)])
    behind = crossed(jnp.stack([sources, beside]), "x", 2)
    tiles = {1: kernel_tiles(1, 0, near, targets, after(beside, pair))}
    block = after(block, tiles[1])
    sent = {q: crossed(block, "x", q) for q in (2, 1, 3)}
    swapped = crossed(block, "c", 1)
    tiles[3] = kernel_tiles(3, 1, near, targets, after(behind[1], swapped))
    base = own_sums(near, targets, sources, block, after(swapped, tiles[3]))
    mine = {q: after(b, base) for q, b in sent.items()}
    other = {q: crossed(b, "c", 1) for q, b in mine.items()}
    sums = {}
    for d in (2, 1, 3, 0):
        made = tiles if d else {1: tiles[1]}
        fused = {2: behind[0]} if d else {2: behind[0], 3: behind[1]}
        part = leaf_sums(d, near, targets, base, made, fused, mine, other)
        sums[d] = moved(part, "y", d) if d else part
    far_sample, inv0, proj0, sq0 = leaf_node([sums[d] for d in range(4)])
    sib = crossed(sq0, "y", 1)
    leaf_basis, carried = carry(far_sample, inv0, proj0)
    inv1, proj1, sq1 = pair_node(sq0, after(sib, carried))
    cousin = crossed(sq1, "y", 2)
    carried = carry2(carried, inv1, proj1)
    nested = last_node(sq1, cousin, carried)
    return (leaf_basis, nested)


def solution(mesh):
    torus = Mesh(mesh.devices.reshape(8, 2, 4, 4), ("z", "c", "x", "y"))
    return jax.shard_map(
        per_device,
        mesh=torus,
        in_specs=(P(None, ROW), P(None, COL), P(COL, ROW), P(ROW, None)),
        out_specs=(P(ROW + COL, None), P(ROW + COL, None)),
        check_vma=False,
    )
```

```python
import functools

import jax
import jax.numpy as jnp
from jax import lax
from jax.sharding import Mesh
from jax.sharding import PartitionSpec as P
from jax.experimental import pallas as pl
from jax.experimental.pallas import tpu as pltpu


LEAF = 512
corr_length = 0.1
ridge = 0.1
LOG2E = 1.4426950408889634
HI = lax.Precision.HIGHEST
F32 = jnp.float32
BF = jnp.bfloat16


def parts3(x):
    a = x.astype(BF).astype(F32)
    rest = x - a
    b = rest.astype(BF).astype(F32)
    return a, b, rest - b


def features(pts_ref, centre, source, masked=0.0):
    points = pts_ref[...]
    row = lax.broadcasted_iota(jnp.int32, points.shape, 0)
    shift = jnp.where(row < 3, (points - centre) * (LOG2E / corr_length), 0.0)
    norm = jnp.sum(shift * shift, axis=0, keepdims=True) + masked
    if source:
        a, b, c = parts3(jnp.where(row == 3, norm, jnp.where(row == 4, 1.0, shift)))
        stack = [a, b, a, c, b, a]
    else:
        a, b, c = parts3(jnp.where(row == 4, norm, jnp.where(row == 3, 1.0, -2.0 * shift)))
        stack = [a, a, b, a, b, c]
    return jnp.concatenate(stack, axis=0).astype(BF)


def kernel_tile(rows, cols):
    d2 = lax.dot_general(rows, cols, (((0,), (0,)), ((), ())), preferred_element_type=F32)
    d2 = jnp.maximum(d2, 1e-24)
    return jnp.exp2(-(d2 * lax.rsqrt(d2))).astype(BF)


def target_features(tgt_ref, pts_ref, row_leaf):
    pts_ref[...] = jnp.zeros_like(pts_ref)
    pts_ref[0:3, :] = tgt_ref[:, pl.ds(pl.multiple_of(row_leaf * LEAF, LEAF), LEAF)]
    centre = jnp.mean(pts_ref[...], axis=1, keepdims=True)
    return features(pts_ref, centre, False), centre


def place():
    return [lax.axis_index(a) for a in ("z", "c", "x", "y")]


def tile_of(q, i, leaf, near_ref, src_ref, pts_ref, cols, centre):
    _, _, x, y = place()
    leaf_id = (jnp.bitwise_xor(x, q) * 4 + y) * 4 + i
    hit = near_ref[0, x * 4 + leaf] == leaf_id
    for k in range(1, 8):
        hit = jnp.logical_or(hit, near_ref[k, x * 4 + leaf] == leaf_id)
    pts_ref[0:3, :] = src_ref[:, i * LEAF:(i + 1) * LEAF]
    return kernel_tile(features(pts_ref, centre, True, jnp.where(hit, 1e9, 0.0)), cols)


def tiles_body(q, first, end, near_ref, tgt_ref, src_ref, out_ref, tpts_ref, spts_ref):
    _, _, x, y = place()
    spts_ref[...] = jnp.zeros_like(spts_ref)

    def one_leaf(turn, carry):
        leaf = jnp.bitwise_and(y + turn, 3)
        cols, centre = target_features(tgt_ref, tpts_ref, x * 4 + leaf)
        for i in range(4):
            out_ref[turn - first, i * LEAF:(i + 1) * LEAF, :] = tile_of(
                q, i, leaf, near_ref, src_ref, spts_ref.at[i], cols, centre)
        return carry

    lax.fori_loop(first, end, one_leaf, 0)


def params():
    return pltpu.CompilerParams(vmem_limit_bytes=16 * 2**20)


def kernel_tiles(q, first, end, near, targets, sources):
    vm = pl.BlockSpec(memory_space=pltpu.VMEM)
    return pl.pallas_call(
        functools.partial(tiles_body, q, first, end),
        out_shape=jax.ShapeDtypeStruct((end - first, 2048, LEAF), BF),
        in_specs=[pl.BlockSpec(memory_space=pltpu.SMEM), vm, vm],
        out_specs=vm,
        scratch_shapes=[pltpu.VMEM((8, LEAF), F32), pltpu.VMEM((4, 8, LEAF), F32)],
        cost_estimate=pl.CostEstimate(flops=8_000_000_000, bytes_accessed=8_400_000, transcendentals=8_400_000),
        compiler_params=params(),
        name="kernel_tiles",
    )(near, targets, sources)


def own_body(near_ref, tgt_ref, src_ref, mine_ref, other_ref, out_ref, held_ref, tpts_ref, spts_ref):
    _, _, x, y = place()
    spts_ref[...] = jnp.zeros_like(spts_ref)

    def one_leaf(turn, carry):
        leaf = jnp.bitwise_and(y + turn, 3)
        cols, centre = target_features(tgt_ref, tpts_ref, x * 4 + leaf)
        total = None
        for n in range(2):
            for i in (2 * n, 2 * n + 1):
                held_ref[i * LEAF:(i + 1) * LEAF, :] = tile_of(
                    0, i, leaf, near_ref, src_ref, spts_ref.at[i], cols, centre)
            part = slice(1024 * n, 1024 * (n + 1))
            rows = jnp.concatenate([r[:, :, part].reshape(64, 1024) for r in (mine_ref, other_ref)], axis=0)
            term = jnp.dot(rows, held_ref[part, :], preferred_element_type=F32)
            total = term if total is None else total + term
        out_ref[turn] = total
        return carry

    lax.fori_loop(0, 4, one_leaf, 0)


def own_sums(near, targets, sources, mine, other):
    vm = pl.BlockSpec(memory_space=pltpu.VMEM)
    return pl.pallas_call(
        own_body,
        out_shape=jax.ShapeDtypeStruct((4, 128, LEAF), F32),
        in_specs=[pl.BlockSpec(memory_space=pltpu.SMEM)] + [vm] * 4,
        out_specs=vm,
        scratch_shapes=[pltpu.VMEM((2048, LEAF), BF), pltpu.VMEM((8, LEAF), F32), pltpu.VMEM((4, 8, LEAF), F32)],
        cost_estimate=pl.CostEstimate(flops=8_000_000_000, bytes_accessed=8_400_000, transcendentals=8_400_000),
        compiler_params=params(),
        name="own_sums",
    )(near, targets, sources, mine, other)


def sums_body(turn, stored, fused, places, near_ref, tgt_ref, base_ref, *refs):
    ns, nf = len(stored), len(fused)
    tiles, refs = refs[:ns], refs[ns:]
    srcs, refs = refs[:nf], refs[nf:]
    mine, refs = refs[:ns + nf], refs[ns + nf:]
    other, refs = refs[:ns + nf], refs[ns + nf:]
    out_ref, held_ref, tpts_ref, spts_ref = refs
    _, _, x, y = place()
    leaf = jnp.bitwise_and(y + turn, 3)
    cols, centre = target_features(tgt_ref, tpts_ref, x * 4 + leaf)
    spts_ref[...] = jnp.zeros_like(spts_ref)
    total = base_ref[turn]
    for n in range(ns + nf):
        rows = jnp.concatenate([mine[n][...].reshape(64, 2048), other[n][...].reshape(64, 2048)], axis=0)
        if n >= ns:
            for i in range(4):
                held_ref[n - ns, i * LEAF:(i + 1) * LEAF, :] = tile_of(
                    fused[n - ns], i, leaf, near_ref, srcs[n - ns], spts_ref.at[4 * (n - ns) + i], cols, centre)
            tile = held_ref[n - ns]
        else:
            tile = tiles[n][places[n]]
        total = total + jnp.dot(rows, tile, preferred_element_type=F32)
    out_ref[...] = total


def leaf_sums(turn, near, targets, base, tiles, sources, mine, other):
    stored, fused = sorted(tiles), sorted(sources)
    order = stored + fused
    vm = pl.BlockSpec(memory_space=pltpu.VMEM)
    sm = pl.BlockSpec(memory_space=pltpu.SMEM)
    return pl.pallas_call(
        functools.partial(sums_body, turn, stored, fused, [tiles[q][1] for q in stored]),
        out_shape=jax.ShapeDtypeStruct((128, LEAF), F32),
        in_specs=[sm, vm, vm] + [vm] * (3 * (len(stored) + len(fused))),
        scratch_shapes=[
            pltpu.VMEM((len(fused), 2048, LEAF), BF),
            pltpu.VMEM((8, LEAF), F32),
            pltpu.VMEM((4 * len(fused), 8, LEAF), F32),
        ],
        cost_estimate=pl.CostEstimate(flops=4_000_000_000, bytes_accessed=9_000_000, transcendentals=1_000_000),
        compiler_params=params(),
        name="leaf_sums",
    )(near, targets, base, *[tiles[q][0] for q in stored], *[sources[q] for q in fused],
      *[mine[q] for q in order], *[other[q] for q in order])


def spread(x, lane):
    return jnp.take_along_axis(x, jnp.full(x.shape, lane, jnp.int32), axis=1, mode="promise_in_bounds")


def row(x, k):
    return jnp.broadcast_to(x[k:k + 1, :], x.shape)


def pivots(cols, k):
    a, off, d = row(cols[k], k), row(cols[k], k + 1), row(cols[k + 1], k + 1)
    inv = lax.rsqrt(a)
    rest = lax.rsqrt(a * d - off * off)
    return (inv, (a * inv) * rest), (inv * inv, a * (rest * rest))


def eliminate(gram, aug_ref, top_ref):
    n = 128
    i = lax.broadcasted_iota(jnp.int32, (n, n), 0)
    j = lax.broadcasted_iota(jnp.int32, (n, n), 1)
    aug_ref[:, :n] = gram
    aug_ref[:, n:] = jnp.where(i == j, 1.0, 0.0)
    sub = lax.broadcasted_iota(jnp.int32, (8, n), 0)
    lane = lax.broadcasted_iota(jnp.int32, (8, n), 1)
    for at in range(0, n, 16):
        high = [aug_ref[at:at + 8, :n], aug_ref[at:at + 8, n:]]
        low = [aug_ref[at + 8:at + 16, :n], aug_ref[at + 8:at + 16, n:]]
        upper = [spread(high[0], at + k) for k in range(8)]
        under = [spread(low[0], at + k) for k in range(8)]
        lower = [spread(low[0], at + 8 + k) for k in range(8)]
        scale_high = scale_low = jnp.zeros((8, n), F32)
        for k in range(0, 8, 2):
            scales, squares = pivots(upper, k)
            scale_high = jnp.where(sub == k, scales[0], jnp.where(sub == k + 1, scales[1], scale_high))
            for p, square in ((k, squares[0]), (k + 1, squares[1])):
                mult = jnp.where(sub > p, upper[p] * square, 0.0)
                wide = under[p] * square
                for q in range(p + 1, 8):
                    entry = row(upper[p], q)
                    upper[q] = upper[q] - mult * entry
                    under[q] = under[q] - wide * entry
                for q in range(8):
                    lower[q] = lower[q] - wide * row(under[p], q)
                for h in range(2):
                    line = row(high[h], p)
                    low[h] = low[h] - wide * line
                    if p < 7:
                        high[h] = high[h] - mult * line
        for k in range(0, 8, 2):
            scales, squares = pivots(lower, k)
            scale_low = jnp.where(sub == k, scales[0], jnp.where(sub == k + 1, scales[1], scale_low))
            for p, square in ((k, squares[0]), (k + 1, squares[1])):
                if p < 7:
                    mult = jnp.where(sub > p, lower[p] * square, 0.0)
                    for q in range(p + 1, 8):
                        lower[q] = lower[q] - mult * row(lower[p], q)
                    for h in range(2):
                        low[h] = low[h] - mult * row(low[h], p)
        left = [jnp.where(lane >= sub + at, high[0] * scale_high, 0.0), jnp.where(lane >= sub + at + 8, low[0] * scale_low, 0.0)]
        right = [high[1] * scale_high, low[1] * scale_low]
        for h in range(2):
            top_ref[at + 8 * h:at + 8 * h + 8, :n] = left[h]
            top_ref[at + 8 * h:at + 8 * h + 8, n:] = right[h]
        if at < n - 16:
            l1, l2, l3 = parts3(jnp.concatenate(left, axis=0))
            r1, r2, r3 = parts3(jnp.concatenate(right, axis=0))
            lhs = jnp.concatenate([l1, l1, l2, l1, l2, l3], axis=0).astype(BF)
            rl = jnp.concatenate([l1, l2, l1, l3, l2, l1], axis=0)
            rr = jnp.concatenate([r1, r2, r1, r3, r2, r1], axis=0)
            rhs = jnp.concatenate([rl, rr], axis=1).astype(BF)
            upd = lax.dot_general(lhs, rhs, (((0,), (0,)), ((), ())), preferred_element_type=F32)
            aug_ref[at + 16:, :] -= upd[at + 16:, :]


def regular(gram):
    i = lax.broadcasted_iota(jnp.int32, gram.shape, 0)
    j = lax.broadcasted_iota(jnp.int32, gram.shape, 1)
    diag = jnp.where(i == j, gram, 0.0)
    mean = jnp.sum(jnp.sum(diag, axis=1, keepdims=True), axis=0, keepdims=True) / gram.shape[0]
    return gram / mean + jnp.where(i == j, ridge, 0.0), mean


def factors(gram, aug_ref, top_ref):
    scaled, mean = regular(gram)
    eliminate(scaled, aug_ref, top_ref)
    inv = top_ref[:, 128:]
    root = lax.rsqrt(mean)
    return inv * root, (top_ref[:, :128] - ridge * inv) * (mean * root)


def tdot(a, b):
    return lax.dot_general(a, b, (((0,), (0,)), ((), ())), precision=HI, preferred_element_type=F32)


def ndot(a, b):
    return lax.dot_general(a, b, (((1,), (1,)), ((), ())), precision=HI, preferred_element_type=F32)


def mdot(a, b):
    return lax.dot_general(a, b, (((1,), (0,)), ((), ())), precision=HI, preferred_element_type=F32)


def leaf_body(a_ref, b_ref, c_ref, d_ref, z_ref, inv_ref, proj_ref, sq_ref, aug_ref, top_ref):
    z, c, _, _ = place()
    for k in range(4):
        for s in range(2):
            plane = jnp.bitwise_and(z - 2 * k - (c if s == 0 else 1 - c), 7)
            rows = slice(64 * s + 16 * k, 64 * s + 16 * k + 16)
            both = (a_ref[rows, :] + b_ref[rows, :]) + (c_ref[rows, :] + d_ref[rows, :])
            z_ref[pl.ds(pl.multiple_of(plane * 16, 16), 16), :] = both
    z = z_ref[...]
    inv, proj = factors(ndot(z, z) * (1.0 / LEAF), aug_ref, top_ref)
    inv_ref[...] = inv
    proj_ref[...] = proj
    sq_ref[...] = tdot(proj, proj)


def node_body(a_ref, b_ref, inv_ref, proj_ref, sq_ref, aug_ref, top_ref):
    inv, proj = factors((a_ref[...] + b_ref[...]) * (1.0 / 256), aug_ref, top_ref)
    inv_ref[...] = inv
    proj_ref[...] = proj
    sq_ref[...] = tdot(proj, proj)


def carry_body(z_ref, inv_ref, proj_ref, base_ref, next_ref):
    base = lax.dot_general(z_ref[...], inv_ref[...], (((0,), (1,)), ((), ())), precision=HI, preferred_element_type=F32)
    base_ref[...] = base
    next_ref[...] = mdot(base, proj_ref[...])


def carry2_body(z_ref, inv_ref, proj_ref, next_ref):
    next_ref[...] = mdot(ndot(z_ref[...], inv_ref[...]), proj_ref[...])


def last_body(a_ref, b_ref, z_ref, out_ref, aug_ref, top_ref):
    inv, _ = factors((a_ref[...] + b_ref[...]) * (1.0 / 256), aug_ref, top_ref)
    out_ref[...] = ndot(z_ref[...], inv) * (1.0 / 128)


def sds(*shape):
    return jax.ShapeDtypeStruct(shape, F32)


SCR = [pltpu.VMEM((128, 256), F32), pltpu.VMEM((128, 256), F32)]


def leaf_node(parts):
    vm = pl.BlockSpec(memory_space=pltpu.VMEM)
    return pl.pallas_call(
        leaf_body,
        out_shape=(sds(128, LEAF),) + (sds(128, 128),) * 3,
        in_specs=[vm] * 4,
        scratch_shapes=SCR,
        name="leaf_node",
        compiler_params=params(),
    )(*parts)


def pair_node(a, b):
    return pl.pallas_call(node_body, out_shape=(sds(128, 128),) * 3, scratch_shapes=SCR, name="pair_node", compiler_params=params())(a, b)


def carry(z, inv, proj):
    return pl.pallas_call(carry_body, out_shape=(sds(512, 128),) * 2, name="carry", compiler_params=params())(z, inv, proj)


def carry2(z, inv, proj):
    return pl.pallas_call(carry2_body, out_shape=sds(512, 128), name="carry2", compiler_params=params())(z, inv, proj)


def last_node(a, b, z):
    return pl.pallas_call(last_body, out_shape=sds(512, 128), scratch_shapes=SCR, name="last_node", compiler_params=params())(a, b, z)


ROW = ("z", "c")
COL = ("x", "y")


def moved(x, axis, by):
    size = lax.axis_size(axis)
    return lax.ppermute(x, axis, [(i, (i + by) % size) for i in range(size)])


def crossed(x, axis, bit):
    return lax.ppermute(x, axis, [(i, i ^ bit) for i in range(lax.axis_size(axis))])


def over_planes(x, even, odd):
    pairs = [(2 * i + c, 2 * ((i + by) % 8) + c) for i in range(8) for c, by in ((0, even), (1, odd)) if by]
    return lax.ppermute(x, ROW, pairs)


def own_planes(samples, core):
    flat = samples.T
    across = crossed(flat, "c", 1)
    own = jnp.where(core == 0, jnp.concatenate([flat, across]), jnp.concatenate([across, flat]))
    behind = [over_planes(own, 2 * k, 2 * k + 1) for k in (1, 2, 3)]
    first = jnp.where(core == 0, own, over_planes(own, None, 1))
    return own, jnp.stack([first] + behind)


def after(x, *work):
    return lax.optimization_barrier((x, *work))[0]


def per_device(targets, sources, samples, near):
    core = lax.axis_index("c")
    near = near.T
    beside = crossed(sources, "x", 1)
    own, block = own_planes(samples, core)
    beside = after(beside, own)
    behind = crossed(jnp.stack([sources, beside]), "x", 2)
    early = kernel_tiles(1, 0, 4, near, targets, beside)
    block = after(block, early)
    sent = {q: crossed(block, "x", q) for q in (2, 1, 3)}
    swapped = crossed(block, "c", 1)
    middle = kernel_tiles(3, 1, 3, near, targets, after(behind[1], swapped))
    base = own_sums(near, targets, sources, block, after(swapped, middle))
    mine = {q: after(b, base) for q, b in sent.items()}
    other, sums = {}, {}
    for q, b in mine.items():
        other[q] = crossed(b, "c", 1)
    late = kernel_tiles(3, 3, 4, near, targets, behind[1])
    for d in (2, 1, 3, 0):
        made = {1: (early, d)}
        fused = {2: behind[0]}
        if d:
            made[3] = (late, 0) if d == 3 else (middle, d - 1)
        else:
            fused[3] = behind[1]
        part = leaf_sums(d, near, targets, base, made, fused, mine, other)
        sums[d] = moved(part, "y", d) if d else part
    far_sample, inv0, proj0, sq0 = leaf_node([sums[d] for d in range(4)])
    sib = crossed(sq0, "y", 1)
    leaf_basis, carried = carry(far_sample, inv0, proj0)
    inv1, proj1, sq1 = pair_node(sq0, after(sib, carried))
    cousin = crossed(sq1, "y", 2)
    carried = carry2(carried, inv1, proj1)
    nested = last_node(sq1, cousin, carried)
    return (leaf_basis, nested)


def solution(mesh):
    torus = Mesh(mesh.devices.reshape(8, 2, 4, 4), ("z", "c", "x", "y"))
    return jax.shard_map(
        per_device,
        mesh=torus,
        in_specs=(P(None, ROW), P(None, COL), P(COL, ROW), P(ROW, None)),
        out_specs=(P(ROW + COL, None), P(ROW + COL, None)),
        check_vma=False,
    )
```

```python
import functools

import jax
import jax.numpy as jnp
from jax import lax
from jax.sharding import Mesh
from jax.sharding import PartitionSpec as P
from jax.experimental import pallas as pl
from jax.experimental.pallas import tpu as pltpu


LEAF = 512
corr_length = 0.1
ridge = 0.1
LOG2E = 1.4426950408889634
HI = lax.Precision.HIGHEST
F32 = jnp.float32
BF = jnp.bfloat16


def parts3(x):
    a = x.astype(BF).astype(F32)
    rest = x - a
    b = rest.astype(BF).astype(F32)
    return a, b, rest - b


def features(pts_ref, centre, source, masked=0.0):
    points = pts_ref[...]
    row = lax.broadcasted_iota(jnp.int32, points.shape, 0)
    shift = jnp.where(row < 3, (points - centre) * (LOG2E / corr_length), 0.0)
    norm = jnp.sum(shift * shift, axis=0, keepdims=True) + masked
    if source:
        a, b, c = parts3(jnp.where(row == 3, norm, jnp.where(row == 4, 1.0, shift)))
        stack = [a, b, a, c, b, a]
    else:
        a, b, c = parts3(jnp.where(row == 4, norm, jnp.where(row == 3, 1.0, -2.0 * shift)))
        stack = [a, a, b, a, b, c]
    return jnp.concatenate(stack, axis=0).astype(BF)


def kernel_tile(rows, cols):
    d2 = lax.dot_general(rows, cols, (((0,), (0,)), ((), ())), preferred_element_type=F32)
    d2 = jnp.maximum(d2, 1e-24)
    return jnp.exp2(-(d2 * lax.rsqrt(d2))).astype(BF)


def target_features(tgt_ref, pts_ref, row_leaf):
    pts_ref[...] = jnp.zeros_like(pts_ref)
    pts_ref[0:3, :] = tgt_ref[:, pl.ds(pl.multiple_of(row_leaf * LEAF, LEAF), LEAF)]
    centre = jnp.mean(pts_ref[...], axis=1, keepdims=True)
    return features(pts_ref, centre, False), centre


def place():
    return [lax.axis_index(a) for a in ("z", "c", "x", "y")]


def tile_of(q, i, leaf, near_ref, src_ref, pts_ref, cols, centre):
    _, _, x, y = place()
    leaf_id = (jnp.bitwise_xor(x, q) * 4 + y) * 4 + i
    hit = near_ref[0, x * 4 + leaf] == leaf_id
    for k in range(1, 8):
        hit = jnp.logical_or(hit, near_ref[k, x * 4 + leaf] == leaf_id)
    pts_ref[0:3, :] = src_ref[:, i * LEAF:(i + 1) * LEAF]
    return kernel_tile(features(pts_ref, centre, True, jnp.where(hit, 1e9, 0.0)), cols)


def tiles_body(q, first, end, near_ref, tgt_ref, src_ref, out_ref, tpts_ref, spts_ref):
    _, _, x, y = place()
    spts_ref[...] = jnp.zeros_like(spts_ref)

    def one_leaf(turn, carry):
        leaf = jnp.bitwise_and(y + turn, 3)
        cols, centre = target_features(tgt_ref, tpts_ref, x * 4 + leaf)
        for i in range(4):
            out_ref[turn - first, i * LEAF:(i + 1) * LEAF, :] = tile_of(
                q, i, leaf, near_ref, src_ref, spts_ref.at[i], cols, centre)
        return carry

    lax.fori_loop(first, end, one_leaf, 0)


def params():
    return pltpu.CompilerParams(vmem_limit_bytes=16 * 2**20)


def kernel_tiles(q, first, end, near, targets, sources):
    vm = pl.BlockSpec(memory_space=pltpu.VMEM)
    return pl.pallas_call(
        functools.partial(tiles_body, q, first, end),
        out_shape=jax.ShapeDtypeStruct((end - first, 2048, LEAF), BF),
        in_specs=[pl.BlockSpec(memory_space=pltpu.SMEM), vm, vm],
        out_specs=vm,
        scratch_shapes=[pltpu.VMEM((8, LEAF), F32), pltpu.VMEM((4, 8, LEAF), F32)],
        cost_estimate=pl.CostEstimate(flops=8_000_000_000, bytes_accessed=8_400_000, transcendentals=8_400_000),
        compiler_params=params(),
        name="kernel_tiles",
    )(near, targets, sources)


def own_body(near_ref, tgt_ref, src_ref, mine_ref, other_ref, out_ref, held_ref, tpts_ref, spts_ref):
    _, _, x, y = place()
    spts_ref[...] = jnp.zeros_like(spts_ref)

    def one_leaf(turn, carry):
        leaf = jnp.bitwise_and(y + turn, 3)
        cols, centre = target_features(tgt_ref, tpts_ref, x * 4 + leaf)
        total = None
        for n in range(2):
            for i in (2 * n, 2 * n + 1):
                held_ref[i * LEAF:(i + 1) * LEAF, :] = tile_of(
                    0, i, leaf, near_ref, src_ref, spts_ref.at[i], cols, centre)
            part = slice(1024 * n, 1024 * (n + 1))
            rows = jnp.concatenate([r[:, :, part].reshape(64, 1024) for r in (mine_ref, other_ref)], axis=0)
            term = jnp.dot(rows, held_ref[part, :], preferred_element_type=F32)
            total = term if total is None else total + term
        out_ref[turn] = total
        return carry

    lax.fori_loop(0, 4, one_leaf, 0)


def own_sums(near, targets, sources, mine, other):
    vm = pl.BlockSpec(memory_space=pltpu.VMEM)
    return pl.pallas_call(
        own_body,
        out_shape=jax.ShapeDtypeStruct((4, 128, LEAF), F32),
        in_specs=[pl.BlockSpec(memory_space=pltpu.SMEM)] + [vm] * 4,
        out_specs=vm,
        scratch_shapes=[pltpu.VMEM((2048, LEAF), BF), pltpu.VMEM((8, LEAF), F32), pltpu.VMEM((4, 8, LEAF), F32)],
        cost_estimate=pl.CostEstimate(flops=8_000_000_000, bytes_accessed=8_400_000, transcendentals=8_400_000),
        compiler_params=params(),
        name="own_sums",
    )(near, targets, sources, mine, other)


def sums_body(turn, stored, fused, places, near_ref, tgt_ref, base_ref, *refs):
    ns, nf = len(stored), len(fused)
    tiles, refs = refs[:ns], refs[ns:]
    srcs, refs = refs[:nf], refs[nf:]
    mine, refs = refs[:ns + nf], refs[ns + nf:]
    other, refs = refs[:ns + nf], refs[ns + nf:]
    out_ref, held_ref, tpts_ref, spts_ref = refs
    _, _, x, y = place()
    leaf = jnp.bitwise_and(y + turn, 3)
    cols, centre = target_features(tgt_ref, tpts_ref, x * 4 + leaf)
    spts_ref[...] = jnp.zeros_like(spts_ref)
    total = base_ref[turn]
    for n in range(ns + nf):
        rows = jnp.concatenate([mine[n][...].reshape(64, 2048), other[n][...].reshape(64, 2048)], axis=0)
        if n >= ns:
            for i in range(4):
                held_ref[n - ns, i * LEAF:(i + 1) * LEAF, :] = tile_of(
                    fused[n - ns], i, leaf, near_ref, srcs[n - ns], spts_ref.at[4 * (n - ns) + i], cols, centre)
            tile = held_ref[n - ns]
        else:
            tile = tiles[n][places[n]]
        total = total + jnp.dot(rows, tile, preferred_element_type=F32)
    out_ref[...] = total


def leaf_sums(turn, near, targets, base, tiles, sources, mine, other):
    stored, fused = sorted(tiles), sorted(sources)
    order = stored + fused
    vm = pl.BlockSpec(memory_space=pltpu.VMEM)
    sm = pl.BlockSpec(memory_space=pltpu.SMEM)
    return pl.pallas_call(
        functools.partial(sums_body, turn, stored, fused, [tiles[q][1] for q in stored]),
        out_shape=jax.ShapeDtypeStruct((128, LEAF), F32),
        in_specs=[sm, vm, vm] + [vm] * (3 * (len(stored) + len(fused))),
        scratch_shapes=[
            pltpu.VMEM((len(fused), 2048, LEAF), BF),
            pltpu.VMEM((8, LEAF), F32),
            pltpu.VMEM((4 * len(fused), 8, LEAF), F32),
        ],
        cost_estimate=pl.CostEstimate(flops=4_000_000_000, bytes_accessed=9_000_000, transcendentals=1_000_000),
        compiler_params=params(),
        name="leaf_sums",
    )(near, targets, base, *[tiles[q][0] for q in stored], *[sources[q] for q in fused],
      *[mine[q] for q in order], *[other[q] for q in order])


def spread(x, lane):
    return jnp.take_along_axis(x, jnp.full(x.shape, lane, jnp.int32), axis=1, mode="promise_in_bounds")


def row(x, k):
    return jnp.broadcast_to(x[k:k + 1, :], x.shape)


def pivots(cols, k):
    a, off, d = row(cols[k], k), row(cols[k], k + 1), row(cols[k + 1], k + 1)
    inv = lax.rsqrt(a)
    rest = lax.rsqrt(a * d - off * off)
    return (inv, (a * inv) * rest), (inv * inv, a * (rest * rest))


def one_round(at, aug_ref, top_ref):
    n = 128
    sub = lax.broadcasted_iota(jnp.int32, (8, n), 0)
    lane = lax.broadcasted_iota(jnp.int32, (8, n), 1)
    high = [aug_ref[at:at + 8, :n], aug_ref[at:at + 8, n:]]
    low = [aug_ref[at + 8:at + 16, :n], aug_ref[at + 8:at + 16, n:]]
    upper = [spread(high[0], at + k) for k in range(8)]
    under = [spread(low[0], at + k) for k in range(8)]
    lower = [spread(low[0], at + 8 + k) for k in range(8)]
    scale_high = scale_low = jnp.zeros((8, n), F32)
    for k in range(0, 8, 2):
        scales, squares = pivots(upper, k)
        scale_high = jnp.where(sub == k, scales[0], jnp.where(sub == k + 1, scales[1], scale_high))
        for p, square in ((k, squares[0]), (k + 1, squares[1])):
            mult = jnp.where(sub > p, upper[p] * square, 0.0)
            wide = under[p] * square
            for q in range(p + 1, 8):
                entry = row(upper[p], q)
                upper[q] = upper[q] - mult * entry
                under[q] = under[q] - wide * entry
            for q in range(8):
                lower[q] = lower[q] - wide * row(under[p], q)
            for h in range(2):
                line = row(high[h], p)
                low[h] = low[h] - wide * line
                if p < 7:
                    high[h] = high[h] - mult * line
    for k in range(0, 8, 2):
        scales, squares = pivots(lower, k)
        scale_low = jnp.where(sub == k, scales[0], jnp.where(sub == k + 1, scales[1], scale_low))
        for p, square in ((k, squares[0]), (k + 1, squares[1])):
            if p < 7:
                mult = jnp.where(sub > p, lower[p] * square, 0.0)
                for q in range(p + 1, 8):
                    lower[q] = lower[q] - mult * row(lower[p], q)
                for h in range(2):
                    low[h] = low[h] - mult * row(low[h], p)
    left = [jnp.where(lane >= sub + at, high[0] * scale_high, 0.0), jnp.where(lane >= sub + at + 8, low[0] * scale_low, 0.0)]
    right = [high[1] * scale_high, low[1] * scale_low]
    for h in range(2):
        top_ref[at + 8 * h:at + 8 * h + 8, :n] = left[h]
        top_ref[at + 8 * h:at + 8 * h + 8, n:] = right[h]
    if at < n - 16:
        l1, l2, l3 = parts3(jnp.concatenate(left, axis=0))
        r1, r2, r3 = parts3(jnp.concatenate(right, axis=0))
        lhs = jnp.concatenate([l1, l1, l2, l1, l2, l3], axis=0).astype(BF)
        rl = jnp.concatenate([l1, l2, l1, l3, l2, l1], axis=0)
        rr = jnp.concatenate([r1, r2, r1, r3, r2, r1], axis=0)
        rhs = jnp.concatenate([rl, rr], axis=1).astype(BF)
        upd = lax.dot_general(lhs, rhs, (((0,), (0,)), ((), ())), preferred_element_type=F32)
        aug_ref[at + 16:, :] -= upd[at + 16:, :]


def eliminate(grams, augs, tops):
    n = 128
    i = lax.broadcasted_iota(jnp.int32, (n, n), 0)
    j = lax.broadcasted_iota(jnp.int32, (n, n), 1)
    for gram, aug_ref in zip(grams, augs):
        aug_ref[:, :n] = gram
        aug_ref[:, n:] = jnp.where(i == j, 1.0, 0.0)
    for at in range(0, n, 16):
        for aug_ref, top_ref in zip(augs, tops):
            one_round(at, aug_ref, top_ref)


def regular(gram):
    i = lax.broadcasted_iota(jnp.int32, gram.shape, 0)
    j = lax.broadcasted_iota(jnp.int32, gram.shape, 1)
    diag = jnp.where(i == j, gram, 0.0)
    mean = jnp.sum(jnp.sum(diag, axis=1, keepdims=True), axis=0, keepdims=True) / gram.shape[0]
    return gram / mean + jnp.where(i == j, ridge, 0.0), mean


def factors(grams, augs, tops):
    scaled, means = zip(*[regular(gram) for gram in grams])
    eliminate(scaled, augs, tops)
    found = []
    for mean, top_ref in zip(means, tops):
        inv, root = top_ref[:, 128:], lax.rsqrt(mean)
        found.append((inv * root, (top_ref[:, :128] - ridge * inv) * (mean * root)))
    return found


def tdot(a, b):
    return lax.dot_general(a, b, (((0,), (0,)), ((), ())), precision=HI, preferred_element_type=F32)


def ndot(a, b):
    return lax.dot_general(a, b, (((1,), (1,)), ((), ())), precision=HI, preferred_element_type=F32)


def mdot(a, b):
    return lax.dot_general(a, b, (((1,), (0,)), ((), ())), precision=HI, preferred_element_type=F32)


def leaf_body(a_ref, b_ref, c_ref, d_ref, z_ref, inv_ref, proj_ref, sq_ref, aug_ref, top_ref):
    z, c, _, _ = place()
    for k in range(4):
        for s in range(2):
            plane = jnp.bitwise_and(z - 2 * k - (c if s == 0 else 1 - c), 7)
            rows = slice(64 * s + 16 * k, 64 * s + 16 * k + 16)
            both = (a_ref[rows, :] + b_ref[rows, :]) + (c_ref[rows, :] + d_ref[rows, :])
            z_ref[pl.ds(pl.multiple_of(plane * 16, 16), 16), :] = both
    z = z_ref[...]
    ((inv, proj),) = factors([ndot(z, z) * (1.0 / LEAF)], [aug_ref], [top_ref])
    inv_ref[...] = inv
    proj_ref[...] = proj
    sq_ref[...] = tdot(proj, proj)


def carry_body(z_ref, inv_ref, proj_ref, base_ref, next_ref):
    base = lax.dot_general(z_ref[...], inv_ref[...], (((0,), (1,)), ((), ())), precision=HI, preferred_element_type=F32)
    base_ref[...] = base
    next_ref[...] = mdot(base, proj_ref[...])


def group_body(own_ref, beside_ref, over_ref, last_ref, z_ref, out_ref, *scratch):
    augs, tops = scratch[:2], scratch[2:]
    (inv, proj), (_, other) = factors(
        [(own_ref[...] + beside_ref[...]) * (1.0 / 256), (over_ref[...] + last_ref[...]) * (1.0 / 256)], augs, tops)
    both = tdot(proj, proj) + tdot(other, other)
    carried = mdot(ndot(z_ref[...], inv), proj)
    ((top_inv, _),) = factors([both * (1.0 / 256)], augs[:1], tops[:1])
    out_ref[...] = ndot(carried, top_inv) * (1.0 / 128)


def sds(*shape):
    return jax.ShapeDtypeStruct(shape, F32)


SCR = [pltpu.VMEM((128, 256), F32), pltpu.VMEM((128, 256), F32)]


def leaf_node(parts):
    vm = pl.BlockSpec(memory_space=pltpu.VMEM)
    return pl.pallas_call(
        leaf_body,
        out_shape=(sds(128, LEAF),) + (sds(128, 128),) * 3,
        in_specs=[vm] * 4,
        scratch_shapes=SCR,
        name="leaf_node",
        compiler_params=params(),
    )(*parts)


def carry(z, inv, proj):
    return pl.pallas_call(carry_body, out_shape=(sds(512, 128),) * 2, name="carry", compiler_params=params())(z, inv, proj)


def group_node(squares, z):
    return pl.pallas_call(group_body, out_shape=sds(512, 128), scratch_shapes=SCR * 2, name="group_node", compiler_params=params())(*squares, z)


ROW = ("z", "c")
COL = ("x", "y")


def moved(x, axis, by):
    size = lax.axis_size(axis)
    return lax.ppermute(x, axis, [(i, (i + by) % size) for i in range(size)])


def crossed(x, axis, bit):
    return lax.ppermute(x, axis, [(i, i ^ bit) for i in range(lax.axis_size(axis))])


def over_planes(x, even, odd):
    pairs = [(2 * i + c, 2 * ((i + by) % 8) + c) for i in range(8) for c, by in ((0, even), (1, odd)) if by]
    return lax.ppermute(x, ROW, pairs)


def own_planes(samples, core):
    flat = samples.T
    across = crossed(flat, "c", 1)
    own = jnp.where(core == 0, jnp.concatenate([flat, across]), jnp.concatenate([across, flat]))
    behind = [over_planes(own, 2 * k, 2 * k + 1) for k in (1, 2, 3)]
    first = jnp.where(core == 0, own, over_planes(own, None, 1))
    return own, jnp.stack([first] + behind)


def after(x, *work):
    return lax.optimization_barrier((x, *work))[0]


def per_device(targets, sources, samples, near):
    core = lax.axis_index("c")
    near = near.T
    beside = crossed(sources, "x", 1)
    own, block = own_planes(samples, core)
    beside = after(beside, own)
    behind = crossed(jnp.stack([sources, beside]), "x", 2)
    early = kernel_tiles(1, 0, 4, near, targets, beside)
    block = after(block, early)
    sent = {q: crossed(block, "x", q) for q in (2, 1, 3)}
    swapped = crossed(block, "c", 1)
    middle = kernel_tiles(3, 1, 3, near, targets, after(behind[1], swapped))
    base = own_sums(near, targets, sources, block, after(swapped, middle))
    mine = {q: after(b, base) for q, b in sent.items()}
    other, sums = {}, {}
    for q, b in mine.items():
        other[q] = crossed(b, "c", 1)
    late = kernel_tiles(3, 3, 4, near, targets, behind[1])
    for d in (2, 1, 3, 0):
        made = {1: (early, d)}
        fused = {2: behind[0]}
        if d:
            made[3] = (late, 0) if d == 3 else (middle, d - 1)
        else:
            fused[3] = behind[1]
        part = leaf_sums(d, near, targets, base, made, fused, mine, other)
        sums[d] = moved(part, "y", d) if d else part
    far_sample, inv0, proj0, sq0 = leaf_node([sums[d] for d in range(4)])
    squares = [sq0] + [crossed(sq0, "y", k) for k in (1, 2, 3)]
    leaf_basis, carried = carry(far_sample, inv0, proj0)
    nested = group_node(squares[:2] + [after(sq, carried) for sq in squares[2:]], carried)
    return (leaf_basis, nested)


def solution(mesh):
    torus = Mesh(mesh.devices.reshape(8, 2, 4, 4), ("z", "c", "x", "y"))
    return jax.shard_map(
        per_device,
        mesh=torus,
        in_specs=(P(None, ROW), P(None, COL), P(COL, ROW), P(ROW, None)),
        out_specs=(P(ROW + COL, None), P(ROW + COL, None)),
        check_vma=False,
    )
```

```python
import functools

import jax
import jax.numpy as jnp
from jax import lax
from jax.sharding import Mesh
from jax.sharding import PartitionSpec as P
from jax.experimental import pallas as pl
from jax.experimental.pallas import tpu as pltpu


LEAF = 512
corr_length = 0.1
ridge = 0.1
LOG2E = 1.4426950408889634
HI = lax.Precision.HIGHEST
F32 = jnp.float32
BF = jnp.bfloat16


def parts3(x):
    a = x.astype(BF).astype(F32)
    rest = x - a
    b = rest.astype(BF).astype(F32)
    return a, b, rest - b


def features(pts_ref, centre, source, masked=0.0):
    points = pts_ref[...]
    row = lax.broadcasted_iota(jnp.int32, points.shape, 0)
    shift = jnp.where(row < 3, (points - centre) * (LOG2E / corr_length), 0.0)
    norm = jnp.sum(shift * shift, axis=0, keepdims=True) + masked
    if source:
        a, b, c = parts3(jnp.where(row == 3, norm, jnp.where(row == 4, 1.0, shift)))
        stack = [a, b, a, c, b, a]
    else:
        a, b, c = parts3(jnp.where(row == 4, norm, jnp.where(row == 3, 1.0, -2.0 * shift)))
        stack = [a, a, b, a, b, c]
    return jnp.concatenate(stack, axis=0).astype(BF)


UNMASKED = (1,)


def kernel_tile(rows, cols):
    d2 = lax.dot_general(rows, cols, (((0,), (0,)), ((), ())), preferred_element_type=F32)
    d2 = jnp.maximum(d2, 1e-24)
    return jnp.exp2(-(d2 * lax.rsqrt(d2))).astype(BF)


def target_features(tgt_ref, pts_ref, row_leaf):
    pts_ref[...] = jnp.zeros_like(pts_ref)
    pts_ref[0:3, :] = tgt_ref[:, pl.ds(pl.multiple_of(row_leaf * LEAF, LEAF), LEAF)]
    centre = jnp.mean(pts_ref[...], axis=1, keepdims=True)
    return features(pts_ref, centre, False), centre


def place():
    return [lax.axis_index(a) for a in ("z", "c", "x", "y")]


def is_near(q, i, leaf, near_ref):
    _, _, x, y = place()
    leaf_id = (jnp.bitwise_xor(x, q) * 4 + y) * 4 + i
    hit = near_ref[0, x * 4 + leaf] == leaf_id
    for k in range(1, 8):
        hit = jnp.logical_or(hit, near_ref[k, x * 4 + leaf] == leaf_id)
    return hit


def tile_of(q, i, leaf, near_ref, src_ref, pts_ref, cols, centre):
    away = 0.0 if near_ref is None else jnp.where(is_near(q, i, leaf, near_ref), 1e9, 0.0)
    pts_ref[0:3, :] = src_ref[:, i * LEAF:(i + 1) * LEAF]
    return kernel_tile(features(pts_ref, centre, True, away), cols)


def tiles_body(q, first, end, *refs):
    near_ref = refs[0] if len(refs) > 5 else None
    tgt_ref, src_ref, out_ref, tpts_ref, spts_ref = refs[-5:]
    _, _, _, y = place()
    spts_ref[...] = jnp.zeros_like(spts_ref)

    def one_leaf(turn, carry):
        leaf = jnp.bitwise_and(y + turn, 3)
        cols, centre = target_features(tgt_ref, tpts_ref, leaf)
        for i in range(4):
            out_ref[turn - first, i * LEAF:(i + 1) * LEAF, :] = tile_of(
                q, i, leaf, near_ref, src_ref, spts_ref.at[i], cols, centre)
        return carry

    lax.fori_loop(first, end, one_leaf, 0)


def params():
    return pltpu.CompilerParams(vmem_limit_bytes=16 * 2**20)


def kernel_tiles(q, first, end, near, targets, sources):
    vm = pl.BlockSpec(memory_space=pltpu.VMEM)
    return pl.pallas_call(
        functools.partial(tiles_body, q, first, end),
        out_shape=jax.ShapeDtypeStruct((end - first, 2048, LEAF), BF),
        in_specs=[pl.BlockSpec(memory_space=pltpu.SMEM)] * (near is not None) + [vm, vm],
        out_specs=vm,
        scratch_shapes=[pltpu.VMEM((8, LEAF), F32), pltpu.VMEM((4, 8, LEAF), F32)],
        cost_estimate=pl.CostEstimate(flops=8_000_000_000, bytes_accessed=8_400_000, transcendentals=8_400_000),
        compiler_params=params(),
        name="kernel_tiles",
    )(*[near] * (near is not None), targets, sources)


def own_body(near_ref, tgt_ref, src_ref, mine_ref, other_ref, out_ref, held_ref, tpts_ref, spts_ref):
    _, _, _, y = place()
    spts_ref[...] = jnp.zeros_like(spts_ref)

    def one_leaf(turn, carry):
        leaf = jnp.bitwise_and(y + turn, 3)
        cols, centre = target_features(tgt_ref, tpts_ref, leaf)
        total = None
        for n in range(2):
            for i in (2 * n, 2 * n + 1):
                held_ref[i * LEAF:(i + 1) * LEAF, :] = tile_of(
                    0, i, leaf, near_ref, src_ref, spts_ref.at[i], cols, centre)
            part = slice(1024 * n, 1024 * (n + 1))
            rows = jnp.concatenate([r[:, :, part].reshape(64, 1024) for r in (mine_ref, other_ref)], axis=0)
            term = jnp.dot(rows, held_ref[part, :], preferred_element_type=F32)
            total = term if total is None else total + term
        out_ref[turn] = total
        return carry

    lax.fori_loop(0, 4, one_leaf, 0)


def own_sums(near, targets, sources, mine, other):
    vm = pl.BlockSpec(memory_space=pltpu.VMEM)
    return pl.pallas_call(
        own_body,
        out_shape=jax.ShapeDtypeStruct((4, 128, LEAF), F32),
        in_specs=[pl.BlockSpec(memory_space=pltpu.SMEM)] + [vm] * 4,
        out_specs=vm,
        scratch_shapes=[pltpu.VMEM((2048, LEAF), BF), pltpu.VMEM((8, LEAF), F32), pltpu.VMEM((4, 8, LEAF), F32)],
        cost_estimate=pl.CostEstimate(flops=8_000_000_000, bytes_accessed=8_400_000, transcendentals=8_400_000),
        compiler_params=params(),
        name="own_sums",
    )(near, targets, sources, mine, other)


def sums_body(turn, stored, fused, places, near_ref, tgt_ref, base_ref, *refs):
    ns, nf = len(stored), len(fused)
    tiles, refs = refs[:ns], refs[ns:]
    srcs, refs = refs[:nf], refs[nf:]
    mine, refs = refs[:ns + nf], refs[ns + nf:]
    other, refs = refs[:ns + nf], refs[ns + nf:]
    out_ref, held_ref, tpts_ref, spts_ref = refs
    _, _, _, y = place()
    leaf = jnp.bitwise_and(y + turn, 3)
    cols, centre = target_features(tgt_ref, tpts_ref, leaf)
    spts_ref[...] = jnp.zeros_like(spts_ref)
    total = base_ref[turn]
    for n in range(ns + nf):
        rows = jnp.concatenate([mine[n][...].reshape(64, 2048), other[n][...].reshape(64, 2048)], axis=0)
        if n < ns and stored[n] in UNMASKED:
            rows = jnp.concatenate([
                jnp.where(is_near(stored[n], i, leaf, near_ref), 0.0, rows[:, i * LEAF:(i + 1) * LEAF]).astype(BF)
                for i in range(4)], axis=1)
        if n >= ns:
            for i in range(4):
                held_ref[n - ns, i * LEAF:(i + 1) * LEAF, :] = tile_of(
                    fused[n - ns], i, leaf, near_ref, srcs[n - ns], spts_ref.at[4 * (n - ns) + i], cols, centre)
            tile = held_ref[n - ns]
        else:
            tile = tiles[n][places[n]]
        total = total + jnp.dot(rows, tile, preferred_element_type=F32)
    out_ref[...] = total


def leaf_sums(turn, near, targets, base, tiles, sources, mine, other):
    stored, fused = sorted(tiles), sorted(sources)
    order = stored + fused
    vm = pl.BlockSpec(memory_space=pltpu.VMEM)
    sm = pl.BlockSpec(memory_space=pltpu.SMEM)
    return pl.pallas_call(
        functools.partial(sums_body, turn, stored, fused, [tiles[q][1] for q in stored]),
        out_shape=jax.ShapeDtypeStruct((128, LEAF), F32),
        in_specs=[sm, vm, vm] + [vm] * (3 * (len(stored) + len(fused))),
        scratch_shapes=[
            pltpu.VMEM((len(fused), 2048, LEAF), BF),
            pltpu.VMEM((8, LEAF), F32),
            pltpu.VMEM((4 * len(fused), 8, LEAF), F32),
        ],
        cost_estimate=pl.CostEstimate(flops=4_000_000_000, bytes_accessed=9_000_000, transcendentals=1_000_000),
        compiler_params=params(),
        name="leaf_sums",
    )(near, targets, base, *[tiles[q][0] for q in stored], *[sources[q] for q in fused],
      *[mine[q] for q in order], *[other[q] for q in order])


def spread(x, lane):
    return jnp.take_along_axis(x, jnp.full(x.shape, lane, jnp.int32), axis=1, mode="promise_in_bounds")


def row(x, k):
    return jnp.broadcast_to(x[k:k + 1, :], x.shape)


def pivots(cols, k):
    a, off, d = row(cols[k], k), row(cols[k], k + 1), row(cols[k + 1], k + 1)
    inv = lax.rsqrt(a)
    rest = lax.rsqrt(a * d - off * off)
    return (inv, (a * inv) * rest), (inv * inv, a * (rest * rest))


def one_round(at, aug_ref, top_ref):
    n = 128
    sub = lax.broadcasted_iota(jnp.int32, (8, n), 0)
    lane = lax.broadcasted_iota(jnp.int32, (8, n), 1)
    high = [aug_ref[at:at + 8, :n], aug_ref[at:at + 8, n:]]
    low = [aug_ref[at + 8:at + 16, :n], aug_ref[at + 8:at + 16, n:]]
    upper = [spread(high[0], at + k) for k in range(8)]
    under = [spread(low[0], at + k) for k in range(8)]
    lower = [spread(low[0], at + 8 + k) for k in range(8)]
    scale_high = scale_low = jnp.zeros((8, n), F32)
    for k in range(0, 8, 2):
        scales, squares = pivots(upper, k)
        scale_high = jnp.where(sub == k, scales[0], jnp.where(sub == k + 1, scales[1], scale_high))
        for p, square in ((k, squares[0]), (k + 1, squares[1])):
            mult = jnp.where(sub > p, upper[p] * square, 0.0)
            wide = under[p] * square
            for q in range(p + 1, 8):
                entry = row(upper[p], q)
                upper[q] = upper[q] - mult * entry
                under[q] = under[q] - wide * entry
            for q in range(8):
                lower[q] = lower[q] - wide * row(under[p], q)
            for h in range(2):
                line = row(high[h], p)
                low[h] = low[h] - wide * line
                if p < 7:
                    high[h] = high[h] - mult * line
    for k in range(0, 8, 2):
        scales, squares = pivots(lower, k)
        scale_low = jnp.where(sub == k, scales[0], jnp.where(sub == k + 1, scales[1], scale_low))
        for p, square in ((k, squares[0]), (k + 1, squares[1])):
            if p < 7:
                mult = jnp.where(sub > p, lower[p] * square, 0.0)
                for q in range(p + 1, 8):
                    lower[q] = lower[q] - mult * row(lower[p], q)
                for h in range(2):
                    low[h] = low[h] - mult * row(low[h], p)
    left = [jnp.where(lane >= sub + at, high[0] * scale_high, 0.0), jnp.where(lane >= sub + at + 8, low[0] * scale_low, 0.0)]
    right = [high[1] * scale_high, low[1] * scale_low]
    for h in range(2):
        top_ref[at + 8 * h:at + 8 * h + 8, :n] = left[h]
        top_ref[at + 8 * h:at + 8 * h + 8, n:] = right[h]
    if at < n - 16:
        l1, l2, l3 = parts3(jnp.concatenate(left, axis=0))
        r1, r2, r3 = parts3(jnp.concatenate(right, axis=0))
        lhs = jnp.concatenate([l1, l1, l2, l1, l2, l3], axis=0).astype(BF)
        rl = jnp.concatenate([l1, l2, l1, l3, l2, l1], axis=0)
        rr = jnp.concatenate([r1, r2, r1, r3, r2, r1], axis=0)
        rhs = jnp.concatenate([rl, rr], axis=1).astype(BF)
        upd = lax.dot_general(lhs, rhs, (((0,), (0,)), ((), ())), preferred_element_type=F32)
        aug_ref[at + 16:, :] -= upd[at + 16:, :]


def eliminate(grams, augs, tops):
    n = 128
    i = lax.broadcasted_iota(jnp.int32, (n, n), 0)
    j = lax.broadcasted_iota(jnp.int32, (n, n), 1)
    for gram, aug_ref in zip(grams, augs):
        aug_ref[:, :n] = gram
        aug_ref[:, n:] = jnp.where(i == j, 1.0, 0.0)
    for at in range(0, n, 16):
        for aug_ref, top_ref in zip(augs, tops):
            one_round(at, aug_ref, top_ref)


def regular(gram):
    i = lax.broadcasted_iota(jnp.int32, gram.shape, 0)
    j = lax.broadcasted_iota(jnp.int32, gram.shape, 1)
    diag = jnp.where(i == j, gram, 0.0)
    mean = jnp.sum(jnp.sum(diag, axis=1, keepdims=True), axis=0, keepdims=True) / gram.shape[0]
    return gram / mean + jnp.where(i == j, ridge, 0.0), mean


def factors(grams, augs, tops):
    scaled, means = zip(*[regular(gram) for gram in grams])
    eliminate(scaled, augs, tops)
    found = []
    for mean, top_ref in zip(means, tops):
        inv, root = top_ref[:, 128:], lax.rsqrt(mean)
        found.append((inv * root, (top_ref[:, :128] - ridge * inv) * (mean * root)))
    return found


def tdot(a, b):
    return lax.dot_general(a, b, (((0,), (0,)), ((), ())), precision=HI, preferred_element_type=F32)


def ndot(a, b):
    return lax.dot_general(a, b, (((1,), (1,)), ((), ())), precision=HI, preferred_element_type=F32)


def mdot(a, b):
    return lax.dot_general(a, b, (((1,), (0,)), ((), ())), precision=HI, preferred_element_type=F32)


def leaf_body(a_ref, b_ref, c_ref, d_ref, z_ref, inv_ref, proj_ref, sq_ref, aug_ref, top_ref):
    z, c, _, _ = place()
    for k in range(4):
        for s in range(2):
            plane = jnp.bitwise_and(z - 2 * k - (c if s == 0 else 1 - c), 7)
            rows = slice(64 * s + 16 * k, 64 * s + 16 * k + 16)
            both = (a_ref[rows, :] + b_ref[rows, :]) + (c_ref[rows, :] + d_ref[rows, :])
            z_ref[pl.ds(pl.multiple_of(plane * 16, 16), 16), :] = both
    z = z_ref[...]
    ((inv, proj),) = factors([ndot(z, z) * (1.0 / LEAF)], [aug_ref], [top_ref])
    inv_ref[...] = inv
    proj_ref[...] = proj
    sq_ref[...] = tdot(proj, proj)


def carry_body(z_ref, inv_ref, proj_ref, base_ref, next_ref):
    base = lax.dot_general(z_ref[...], inv_ref[...], (((0,), (1,)), ((), ())), precision=HI, preferred_element_type=F32)
    base_ref[...] = base
    next_ref[...] = mdot(base, proj_ref[...])


def group_body(own_ref, beside_ref, over_ref, last_ref, z_ref, out_ref, *scratch):
    augs, tops = scratch[:2], scratch[2:]
    (inv, proj), (_, other) = factors(
        [(own_ref[...] + beside_ref[...]) * (1.0 / 256), (over_ref[...] + last_ref[...]) * (1.0 / 256)], augs, tops)
    both = tdot(proj, proj) + tdot(other, other)
    carried = mdot(ndot(z_ref[...], inv), proj)
    ((top_inv, _),) = factors([both * (1.0 / 256)], augs[:1], tops[:1])
    out_ref[...] = ndot(carried, top_inv) * (1.0 / 128)


def sds(*shape):
    return jax.ShapeDtypeStruct(shape, F32)


SCR = [pltpu.VMEM((128, 256), F32), pltpu.VMEM((128, 256), F32)]


def leaf_node(parts):
    vm = pl.BlockSpec(memory_space=pltpu.VMEM)
    return pl.pallas_call(
        leaf_body,
        out_shape=(sds(128, LEAF),) + (sds(128, 128),) * 3,
        in_specs=[vm] * 4,
        scratch_shapes=SCR,
        name="leaf_node",
        compiler_params=params(),
    )(*parts)


def carry(z, inv, proj):
    return pl.pallas_call(carry_body, out_shape=(sds(512, 128),) * 2, name="carry", compiler_params=params())(z, inv, proj)


def group_node(squares, z):
    return pl.pallas_call(group_body, out_shape=sds(512, 128), scratch_shapes=SCR * 2, name="group_node", compiler_params=params())(*squares, z)


ROW = ("z", "c")
COL = ("x", "y")


def moved(x, axis, by):
    size = lax.axis_size(axis)
    return lax.ppermute(x, axis, [(i, (i + by) % size) for i in range(size)])


def crossed(x, axis, bit):
    return lax.ppermute(x, axis, [(i, i ^ bit) for i in range(lax.axis_size(axis))])


def over_planes(x, even, odd):
    pairs = [(2 * i + c, 2 * ((i + by) % 8) + c) for i in range(8) for c, by in ((0, even), (1, odd)) if by]
    return lax.ppermute(x, ROW, pairs)


def own_planes(samples, core, meanwhile):
    flat = samples.T
    across = after(crossed(flat, "c", 1), meanwhile)
    own = jnp.where(core == 0, jnp.concatenate([flat, across]), jnp.concatenate([across, flat]))
    behind = [over_planes(own, 2 * k, 2 * k + 1) for k in (1, 2, 3)]
    first = jnp.where(core == 0, own, over_planes(own, None, 1))
    return own, jnp.stack([first] + behind)


def after(x, *work):
    return lax.optimization_barrier((x, *work))[0]


def per_device(targets, sources, samples, near):
    core = lax.axis_index("c")
    near = near.T
    beside = crossed(sources, "x", 1)
    targets = lax.dynamic_slice_in_dim(targets, lax.axis_index("x") * 2048, 2048, 1)
    own, block = own_planes(samples, core, targets)
    beside = after(beside, own)
    behind = crossed(jnp.stack([sources, beside]), "x", 2)
    early = kernel_tiles(1, 1, 4, None, targets, beside)
    block = after(block, early)
    sent = {q: crossed(block, "x", q) for q in (2, 1, 3)}
    swapped = crossed(block, "c", 1)
    base = own_sums(near, targets, sources, block, swapped)
    behind = after(behind, base)
    middle = kernel_tiles(3, 1, 3, near, targets, behind[1])
    mine = {q: after(b, middle) for q, b in sent.items()}
    other, sums = {}, {}
    for q, b in mine.items():
        other[q] = crossed(b, "c", 1)
    late = kernel_tiles(3, 3, 4, near, targets, behind[1])
    for d in (2, 1, 3, 0):
        made, fused = {}, {2: behind[0]}
        if d:
            made[1] = (early, d - 1)
            made[3] = (late, 0) if d == 3 else (middle, d - 1)
        else:
            fused.update({1: beside, 3: behind[1]})
        part = leaf_sums(d, near, targets, base, made, fused, mine, other)
        sums[d] = moved(part, "y", d) if d else part
    far_sample, inv0, proj0, sq0 = leaf_node([sums[d] for d in range(4)])
    squares = [sq0] + [crossed(sq0, "y", k) for k in (1, 2, 3)]
    leaf_basis, carried = carry(far_sample, inv0, proj0)
    nested = group_node(squares[:2] + [after(sq, carried) for sq in squares[2:]], carried)
    return (leaf_basis, nested)


def solution(mesh):
    torus = Mesh(mesh.devices.reshape(8, 2, 4, 4), ("z", "c", "x", "y"))
    return jax.shard_map(
        per_device,
        mesh=torus,
        in_specs=(P(None, ROW), P(None, COL), P(COL, ROW), P(ROW, None)),
        out_specs=(P(ROW + COL, None), P(ROW + COL, None)),
        check_vma=False,
    )
```
